512 devices in a mesh: tm: 16 (over z, core), lat: 32 (over x, y).
Axes of the slice: x: 4, y: 8, z: 8, core: 2. Of those that a mesh axis runs over, the one named last changes fastest.
Arguments:
- trajectory: float32 [16, 84, 128, 128], P('tm', None, 'lat'), may hold values from -6 to 6
- step_levels: int32 [17], replicated, may hold values from 0 to 63, as said below
- in_weight: bfloat16 [256, 84], replicated, may hold values from -0.625 to 0.625
- in_bias: float32 [256], replicated, may hold values from -4 to 4
- conv_weight: bfloat16 [2, 256, 2304], replicated, may hold values from -0.125 to 0.125
- cond_weight: bfloat16 [256, 1024], replicated, may hold values from -0.375 to 0.375
- out_weight: bfloat16 [84, 256], replicated, may hold values from -0.375 to 0.375
Outputs:
- advanced: float32 [16, 84, 128, 128], P('tm', None, 'lat')
The draws below stay inside these ranges and needn't reach their ends.
Inputs may be any that keep to these rules, and one draw needn't show every extreme that they name: `step_levels`: strictly increasing; the first entry is 0 and the last is 63.
All inputs are finite; a program needn't handle non-finite values.
Results may differ from the reference program's by a relative error of at most 0.0055.
Values may be sent and summed in bfloat16 or wider, within the bound.
No kernel may reach another device: no remote copies, remote signals or barrier semaphores. Data moves between devices by JAX's collectives and lax.ppermute only.
A program may use at most 64 MiB of HBM per device.

```python
import jax
import jax.numpy as jnp
from jax import lax

C = 84
HID = 256
EMB = 256
LEVELS = 64
ITERS = 2
W = 128
TIMES = 16
LAT = 128


def draw_step_levels(key, part):
    interior = jax.random.permutation(key, LEVELS - 2)[:TIMES - 1] + 1
    interior = jnp.sort(interior.astype(jnp.int32))
    return jnp.concatenate([jnp.zeros((1,), jnp.int32), interior, jnp.full((1,), LEVELS - 1, jnp.int32)])


def block_levels(own_key, shape, shards, least, largest):
    def one(dim, parts):
        steps = jax.random.uniform(jax.random.fold_in(jax.random.fold_in(own_key, 6), dim), (parts,), jnp.float32, least / len(shards), largest / len(shards))
        return jnp.repeat(jnp.exp(steps), shape[dim] // parts).reshape((-1,) + (1,) * (len(shape) - dim - 1))

    loudness = one(*shards[0])
    for cut in shards[1:]:
        loudness = loudness * one(*cut)
    return loudness


def normal_values(stream_key, dims, scale, most, cuts=(), dtype=jnp.bfloat16):
    array = jax.random.normal(stream_key, dims, jnp.float32) * scale
    if len(cuts) > 0:
        array = block_levels(stream_key, dims, cuts, -0.22, 0.18) * array
    return jnp.clip(array, min=-most, max=most).astype(dtype)


def setup_inputs(seed: int = 0) -> dict:
    key_list = jax.random.split(jax.random.key(seed), 8)
    trajectory = normal_values(key_list[0], (TIMES, C, LAT, W), 1.0, 6.0, ((0, 16), (2, 32)), jnp.float32)
    step_levels = draw_step_levels(jax.random.fold_in(key_list[7], 71), 0)
    in_weight = normal_values(key_list[2], (HID, C), C ** -0.5, 0.625)
    in_bias = normal_values(key_list[3], (HID,), 1.0, 4.0, (), jnp.float32)
    conv_weight = normal_values(key_list[4], (2, HID, 9 * HID), (9 * HID) ** -0.5, 0.125)
    cond_weight = normal_values(key_list[5], (EMB, 4 * HID), EMB ** -0.5, 0.375)
    out_weight = normal_values(key_list[6], (C, HID), HID ** -0.5, 0.375)
    return dict(trajectory=trajectory, step_levels=step_levels, in_weight=in_weight, in_bias=in_bias, conv_weight=conv_weight, cond_weight=cond_weight, out_weight=out_weight)


sigma_top = 1.0
sigma_low = 0.02
rho_power = 7.0

def level_sigma(levels):
    fraction = levels.astype(jnp.float32) / (LEVELS - 1)
    root_value = sigma_top ** (1.0 / rho_power) + fraction * (sigma_low ** (1.0 / rho_power) - sigma_top ** (1.0 / rho_power))
    return root_value ** rho_power

def conditions_of(sigma_now, cond_weight):
    freq_count = EMB // 2
    frequency = 100.0 ** (jnp.arange(freq_count).astype(jnp.float32) / freq_count)
    phases = jnp.log(sigma_now) / 4.0 * frequency
    embedding = jnp.concatenate([jnp.cos(phases), jnp.sin(phases)]).astype(jnp.bfloat16)[None, :]
    conditions = jnp.dot(embedding, cond_weight, preferred_element_type=jnp.float32)[0]
    return jnp.split(conditions, 4)

def convolve(padded, weight):
    row_count = padded.shape[1] - 2
    shifted = []
    for offset_row in range(3):
        for offset_col in (-1, 0, 1):
            shifted.append(jnp.roll(padded[:, offset_row:offset_row + row_count, :], -offset_col, axis=2))
    columns_all = jnp.concatenate(shifted, axis=0)
    channels = columns_all.shape[0]
    flattened = columns_all.reshape(channels, -1)
    response = jnp.dot(weight, flattened, preferred_element_type=jnp.float32)
    return response.reshape(weight.shape[0], row_count, padded.shape[2])

def drift_one(current, sigma_now, sigma_next, in_weight, in_bias, conv_weight, cond_weight, out_weight):
    scale_one, shift_one, scale_two, shift_two = conditions_of(sigma_now, cond_weight)
    variance = sigma_now * sigma_now + 0.25
    scaled = (current / jnp.sqrt(variance)).astype(jnp.bfloat16)
    channels, row_count, columns = current.shape
    hidden_zero = jnp.dot(in_weight, scaled.reshape(channels, -1), preferred_element_type=jnp.float32) + in_bias[:, None]
    hidden_zero = hidden_zero.reshape(-1, row_count, columns).astype(jnp.bfloat16)
    pad_rows = ((0, 0), (1, 1), (0, 0))
    response = convolve(jnp.pad(hidden_zero, pad_rows), conv_weight[0])
    hidden_one = jax.nn.silu(response * (1.0 + scale_one[:, None, None]) + shift_one[:, None, None]).astype(jnp.bfloat16)
    response = convolve(jnp.pad(hidden_one, pad_rows), conv_weight[1])
    hidden_two = hidden_one.astype(jnp.float32) + jax.nn.silu(response * (1.0 + scale_two[:, None, None]) + shift_two[:, None, None])
    hidden_two = hidden_two.astype(jnp.bfloat16)
    network = jnp.dot(out_weight, hidden_two.reshape(hidden_two.shape[0], -1), preferred_element_type=jnp.float32)
    network = network.reshape(channels, row_count, columns)
    denoised = 0.25 / variance * current + 0.5 * sigma_now / jnp.sqrt(variance) * network
    return (current - denoised) * ((sigma_next - sigma_now) / sigma_now)

def reference(trajectory, step_levels, in_weight, in_bias, conv_weight, cond_weight, out_weight):
    sigmas = level_sigma(step_levels)
    sigma_list = sigmas[:-1]
    next_list = sigmas[1:]
    first_state = trajectory[0]

    def all_drifts(states):

        def single(members):
            return drift_one(members[0], members[1], members[2], in_weight, in_bias, conv_weight, cond_weight, out_weight)
        return lax.map(single, (states, sigma_list, next_list))
    states = trajectory
    for sweep in range(ITERS - 1):
        drifts = all_drifts(states)
        summed = first_state[None] + jnp.cumsum(drifts, axis=0)
        states = jnp.concatenate([first_state[None], summed[:-1]], axis=0)
    drifts = all_drifts(states)
    return first_state[None] + jnp.cumsum(drifts, axis=0)
```

```python
import functools

import jax
import jax.numpy as jnp
from jax import lax
from jax.experimental import pallas as pl
from jax.experimental.pallas import tpu as pltpu
from jax.sharding import PartitionSpec as P

LEVELS = 64
C = 84
HID = 256
SLOTS = 16
ROWS = 4
COLS = 8
PIECE = 48

SIGMA_TOP = 1.0
SIGMA_LOW = 0.02
RHO = 7.0
ROOT_TOP = SIGMA_TOP ** (1.0 / RHO)
ROOT_LOW = SIGMA_LOW ** (1.0 / RHO)

F32 = jnp.float32
BF16 = jnp.bfloat16
VMEM = pltpu.VMEM
NT = (((1,), (1,)), ((), ()))
TN = (((0,), (0,)), ((), ()))


def iota(shape, dim):
    return lax.broadcasted_iota(jnp.int32, shape, dim)


def one_hot(mask):
    return jnp.where(mask, 1.0, 0.0).astype(BF16)


def sigma_of(level):
    root = ROOT_TOP + level.astype(F32) / (LEVELS - 1) * (ROOT_LOW - ROOT_TOP)
    square = root * root
    return square * square * square * root


def lane_of(channel, row):
    head = channel + jnp.where(row >= 2, 64, 0)
    tail = 128 + 32 * row + (channel - 64)
    return jnp.where(channel < 64, head, tail)


def pack_kernel(levels_ref, x_ref, o_ref):
    slot = lax.axis_index("tm")
    level = levels_ref[slot]
    sigma = sigma_of(jnp.full((1, 128), level, jnp.int32))
    scale = jnp.sqrt(sigma * sigma + 0.25)
    scaled = pltpu.roll(x_ref[...] / scale, 4, 1).astype(BF16)
    shape = (C * ROWS, 3 * 128)
    index, lane = iota(shape, 0), iota(shape, 1)
    channel, row = index >> 2, index & 3
    target = lane_of(channel, row)
    target = jnp.where(target < 128, target + 128 * (row & 1), target + 128)
    packed = lax.dot_general(scaled, one_hot(lane == target), TN, preferred_element_type=F32)
    for window in range(SLOTS):
        start = COLS * window
        if window < SLOTS - 1:
            part = packed[start : start + 2 * COLS]
        else:
            part = jnp.concatenate([packed[start:], packed[:COLS]], axis=0)
        part = part.astype(BF16)
        for group in range(3):
            o_ref[window, 16 * group : 16 * group + 16, :] = part[:, 128 * group : 128 * group + 128]


def pack(levels, x):
    return pl.pallas_call(
        pack_kernel,
        out_shape=jax.ShapeDtypeStruct((SLOTS, PIECE, 128), BF16),
        in_specs=[pl.BlockSpec(memory_space=pltpu.SMEM), pl.BlockSpec(memory_space=VMEM)],
        out_specs=pl.BlockSpec(memory_space=VMEM),
        name="pack",
    )(levels, x)


def tables_kernel(now_ref, next_ref, in_w_ref, cond_ref, out_w_ref, film_ref, coef_ref, in_pack_ref, pick_ref, in_t_ref, out_t_ref):
    now, following = sigma_of(now_ref[...]), sigma_of(next_ref[...])
    variance = now * now + 0.25
    root = jnp.sqrt(variance)
    ratio = (following - now) / now
    coef_ref[0] = 1.0 / root
    coef_ref[1] = root
    coef_ref[2] = (1.0 - 0.25 / variance) * ratio
    coef_ref[3] = 0.5 * now / root * ratio
    j = iota((SLOTS, 128), 1).astype(F32)
    frequency = jnp.exp(j * (jnp.log(F32(100.0)) / 128.0))
    phases = jnp.log(now) / 4.0 * frequency
    embedding = jnp.concatenate([jnp.cos(phases), jnp.sin(phases)], axis=1).astype(BF16)
    conditions = jnp.dot(embedding, cond_ref[...], preferred_element_type=F32)
    film_ref[0] = 0.5 * (1.0 + conditions[:, 0:256])
    film_ref[1] = 0.5 * conditions[:, 256:512]
    film_ref[2] = 0.5 * (1.0 + conditions[:, 512:768])
    film_ref[3] = 0.5 * conditions[:, 768:1024]
    channel, lane = iota((128, 256), 0), iota((128, 256), 1)
    in_w = in_w_ref[...]
    for row in range(ROWS):
        pick = one_hot((lane == lane_of(channel, row)) & (channel < C))
        pick_ref[row] = pick
        in_pack_ref[row] = jnp.dot(in_w, pick[:C], preferred_element_type=F32).astype(BF16)
    eye = one_hot((iota((C, 128), 0) == iota((C, 128), 1)))
    in_t_ref[...] = jnp.dot(in_w, eye, preferred_element_type=F32).astype(BF16)
    out_t_ref[...] = lax.dot_general(eye, out_w_ref[...], TN, preferred_element_type=F32).astype(BF16)


def tables(now, following, in_weight, cond_weight, out_weight):
    return pl.pallas_call(
        tables_kernel,
        out_shape=[
            jax.ShapeDtypeStruct((4, SLOTS, HID), F32),
            jax.ShapeDtypeStruct((4, SLOTS, 128), F32),
            jax.ShapeDtypeStruct((ROWS, HID, 256), BF16),
            jax.ShapeDtypeStruct((ROWS, 128, 256), BF16),
            jax.ShapeDtypeStruct((HID, 128), BF16),
            jax.ShapeDtypeStruct((128, HID), BF16),
        ],
        in_specs=[pl.BlockSpec(memory_space=VMEM)] * 5,
        out_specs=[pl.BlockSpec(memory_space=VMEM)] * 6,
        name="tables",
    )(now, following, in_weight, cond_weight, out_weight)


def split(value):
    high = value.astype(BF16)
    return high, (value - high.astype(F32)).astype(BF16)


def taps(ref, row, pitch, start, count):
    parts = []
    for a in (-1, 0, 1):
        for b in (-1, 0, 1):
            parts.append(ref[pl.ds((row + a) * pitch + start + 16 * b, count), :])
    return jnp.concatenate(parts, axis=1)


def film(response, scale, shift):
    cells = response.shape[0] // SLOTS
    half = response.reshape(cells, SLOTS, HID) * scale[None] + shift[None]
    return (half * jnp.tanh(half) + half).reshape(cells * SLOTS, HID)


def main_kernel(low_ref, own_ref, high_ref, film_ref, coef_ref, in_pack_ref, pick_ref, in_t_ref, out_t_ref, bias_ref, conv_ref, o_ref, h0, h1, g0, g1, x1, s2):
    place = lax.axis_index("lat")
    count = lax.axis_size("lat")
    inside_low = jnp.where(place > 0, 1.0, 0.0).astype(F32)
    inside_high = jnp.where(place < count - 1, 1.0, 0.0).astype(F32)
    blocks = (low_ref, own_ref, high_ref)
    gates = (inside_low, F32(1.0), inside_high)
    bias = bias_ref[...]

    shape = (256, 256)
    to, frm = iota(shape, 0), iota(shape, 1)
    swap = one_hot(((to >> 4) == (frm & 15)) & ((to & 15) == (frm >> 4)))

    packed = []
    for ref in blocks:
        groups = []
        for group in range(3):
            part = ref[:, 16 * group : 16 * group + 16, :].reshape(256, 128)
            groups.append(jnp.dot(swap, part, preferred_element_type=F32).astype(BF16))
        packed.append(groups)
    for row in range(ROWS):
        for at in range(3):
            lhs = jnp.concatenate([packed[at][row & 1], packed[at][2]], axis=1)
            hidden = lax.dot_general(lhs, in_pack_ref[row], NT, preferred_element_type=F32) + bias * gates[at]
            i = 4 * at + row
            h0[256 * i : 256 * i + 256, :] = hidden.astype(BF16)
            if 2 <= i < 10:
                value = lax.dot_general(lhs[32:224], pick_ref[row], NT, preferred_element_type=F32)
                value = value.reshape(12, SLOTS, 128) * coef_ref[1][None]
                x1[192 * (i - 2) : 192 * (i - 2) + 192, :] = value.reshape(192, 128)

    def gate_of(row):
        outside = ((place == 0) & (row < 0)) | ((place == count - 1) & (row >= ROWS))
        return jnp.where(outside, 0.0, 1.0).astype(F32)

    def conv_one(i, _):
        gate = gate_of(i - 4)
        response = lax.dot_general(taps(h0, i, 256, 16, 224), conv_ref[0], NT, preferred_element_type=F32)
        hidden = film(response, film_ref[0] * gate, film_ref[1] * gate)
        h1[pl.ds((i - 1) * 224, 224), :] = hidden.astype(BF16)
        return 0

    lax.fori_loop(1, 11, conv_one, 0, unroll=2)

    to, frm = iota((192, 384), 0), iota((192, 384), 1)
    frm = jnp.where(frm >= 192, frm - 192, frm)
    before = one_hot(((to >> 4) == (frm >> 4)) & ((frm & 15) < (to & 15)))

    def conv_two(i, _):
        gate = gate_of(i - 3)
        response = lax.dot_general(taps(h1, i, 224, 16, 192), conv_ref[1], NT, preferred_element_type=F32)
        hidden = h1[pl.ds(i * 224 + 16, 192), :].astype(F32) + film(response, film_ref[2], film_ref[3])
        network = lax.dot_general(hidden.astype(BF16), out_t_ref[...], NT, preferred_element_type=F32)
        x = x1[pl.ds((i - 1) * 192, 192), :].reshape(12, SLOTS, 128)
        drift = coef_ref[2][None] * x - coef_ref[3][None] * network.reshape(12, SLOTS, 128)
        high, low = split(drift.reshape(192, 128))
        earlier = jnp.dot(before, jnp.concatenate([high, low], axis=0), preferred_element_type=F32)
        state = earlier.reshape(12, SLOTS, 128) + x[:, 0:1, :]
        s2[pl.ds((i - 1) * 192, 192), :] = state.reshape(192, 128)
        scaled = (state * (coef_ref[0] * gate)[None]).reshape(192, 128).astype(BF16)
        hidden = lax.dot_general(scaled, in_t_ref[...], NT, preferred_element_type=F32) + bias * gate
        g0[pl.ds((i - 1) * 192, 192), :] = hidden.astype(BF16)
        return 0

    lax.fori_loop(1, 9, conv_two, 0, unroll=2)

    def conv_three(i, _):
        gate = gate_of(i - 2)
        response = lax.dot_general(taps(g0, i, 192, 16, 160), conv_ref[0], NT, preferred_element_type=F32)
        hidden = film(response, film_ref[0] * gate, film_ref[1] * gate)
        g1[pl.ds((i - 1) * 160, 160), :] = hidden.astype(BF16)
        return 0

    lax.fori_loop(1, 7, conv_three, 0, unroll=2)

    to, frm = iota((128, 512), 0), iota((128, 512), 1)
    part, source = frm >> 7, frm & 127
    same = (to & 7) == (source >> 4)
    upto = (part < 2) & ((source & 15) <= (to >> 3))
    start = (part >= 2) & ((source & 15) == 0)
    gather = one_hot(same & (upto | start))

    for row in range(ROWS):
        response = lax.dot_general(taps(g1, row + 1, 160, 16, 128), conv_ref[1], NT, preferred_element_type=F32)
        hidden = g1[160 * (row + 1) + 16 : 160 * (row + 1) + 144, :].astype(F32) + film(response, film_ref[2], film_ref[3])
        network = lax.dot_general(hidden.astype(BF16), out_t_ref[...], NT, preferred_element_type=F32)
        state = s2[192 * (row + 2) + 32 : 192 * (row + 2) + 160, :].reshape(COLS, SLOTS, 128)
        drift = coef_ref[2][None] * state - coef_ref[3][None] * network.reshape(COLS, SLOTS, 128)
        high, low = split(drift.reshape(128, 128))
        anchor_high, anchor_low = split(state.reshape(128, 128))
        advanced = jnp.dot(gather, jnp.concatenate([high, low, anchor_high, anchor_low], axis=0), preferred_element_type=F32)
        o_ref[:, COLS * row : COLS * row + COLS, :] = advanced.reshape(SLOTS, COLS, 128).astype(BF16)


def main(low, own, high, film_table, coef, in_pack, pick, in_t, out_t, bias, conv_weight):
    return pl.pallas_call(
        main_kernel,
        out_shape=jax.ShapeDtypeStruct((SLOTS, ROWS * COLS, 128), BF16),
        in_specs=[pl.BlockSpec(memory_space=VMEM)] * 11,
        out_specs=pl.BlockSpec(memory_space=VMEM),
        scratch_shapes=[
            VMEM((12 * 256, HID), BF16),
            VMEM((10 * 224, HID), BF16),
            VMEM((8 * 192, HID), BF16),
            VMEM((6 * 160, HID), BF16),
            VMEM((8 * 192, 128), F32),
            VMEM((8 * 192, 128), F32),
        ],
        name="patch",
    )(low, own, high, film_table, coef, in_pack, pick, in_t, out_t, bias, conv_weight)


def unpack_kernel(p_ref, o_ref):
    for row in range(ROWS):
        part = jnp.concatenate(
            [p_ref[w, :, :].astype(F32)[COLS * row : COLS * row + COLS, :] for w in range(SLOTS)], axis=0
        )
        o_ref[pl.ds(row, C, stride=ROWS), :] = part.T[:C]


def unpack(pieces):
    return pl.pallas_call(
        unpack_kernel,
        out_shape=jax.ShapeDtypeStruct((C * ROWS, 128), F32),
        in_specs=[pl.BlockSpec(memory_space=VMEM)],
        out_specs=pl.BlockSpec(memory_space=VMEM),
        name="unpack",
    )(pieces)


def on_device(trajectory, step_levels, in_weight, in_bias, conv_weight, cond_weight, out_weight):
    count = lax.axis_size("lat")
    forward = [(i, i + 1) for i in range(count - 1)]
    backward = [(b, a) for a, b in forward]
    pieces = pack(step_levels, trajectory.reshape(C * ROWS, 128))
    own = lax.all_to_all(pieces, "tm", 0, 0)
    low = lax.ppermute(own, "lat", forward)
    high = lax.ppermute(own, "lat", backward)
    now = jnp.broadcast_to(step_levels[:-1, None], (SLOTS, 128))
    following = jnp.broadcast_to(step_levels[1:, None], (SLOTS, 128))
    prepared = tables(now, following, in_weight, cond_weight, out_weight)
    done = main(low, own, high, *prepared, in_bias[None, :], conv_weight)
    back = lax.all_to_all(done, "tm", 0, 0)
    return unpack(back).reshape(1, C, ROWS, 128)


def solution(mesh):
    in_specs = (P("tm", None, "lat", None), P(), P(), P(), P(), P(), P())
    out_specs = P("tm", None, "lat", None)
    return jax.shard_map(on_device, mesh=mesh, in_specs=in_specs, out_specs=out_specs, check_vma=False)
```

```python
import functools

import jax
import jax.numpy as jnp
from jax import lax
from jax.experimental import pallas as pl
from jax.experimental.pallas import tpu as pltpu
from jax.sharding import PartitionSpec as P

LEVELS = 64
C = 84
HID = 256
SLOTS = 16
ROWS = 4
COLS = 8
PIECE = 48
BACK = 24

SIGMA_TOP = 1.0
SIGMA_LOW = 0.02
RHO = 7.0
ROOT_TOP = SIGMA_TOP ** (1.0 / RHO)
ROOT_LOW = SIGMA_LOW ** (1.0 / RHO)

F32 = jnp.float32
BF16 = jnp.bfloat16
VMEM = pltpu.VMEM
NT = (((1,), (1,)), ((), ()))
TN = (((0,), (0,)), ((), ()))


def iota(shape, dim):
    return lax.broadcasted_iota(jnp.int32, shape, dim)


def one_hot(mask):
    return jnp.where(mask, 1.0, 0.0).astype(BF16)


def sigma_of(level):
    root = ROOT_TOP + level.astype(F32) / (LEVELS - 1) * (ROOT_LOW - ROOT_TOP)
    square = root * root
    return square * square * square * root


def lane_of(channel, row):
    head = channel + jnp.where(row >= 2, 64, 0)
    tail = 128 + 32 * row + (channel - 64)
    return jnp.where(channel < 64, head, tail)


def pack_kernel(levels_hbm, x_hbm, o_ref, levels_ref, x_ref, sems):
    get_levels = pltpu.make_async_copy(levels_hbm, levels_ref, sems.at[0])
    get_x = pltpu.make_async_copy(x_hbm, x_ref, sems.at[1])
    get_levels.start()
    get_x.start()
    slot = lax.axis_index("tm")
    shape = (C * ROWS, 3 * 128)
    index, lane = iota(shape, 0), iota(shape, 1)
    channel, row = index >> 2, index & 3
    target = lane_of(channel, row)
    target = jnp.where(target < 128, target + 128 * (row & 1), target + 128)
    places = one_hot(lane == target)
    get_levels.wait()
    sigma = sigma_of(jnp.full((1, 128), levels_ref[slot], jnp.int32))
    scale = jnp.sqrt(sigma * sigma + 0.25)
    get_x.wait()
    scaled = pltpu.roll(x_ref[...] / scale, 4, 1).astype(BF16)
    packed = lax.dot_general(scaled, places, TN, preferred_element_type=F32)
    for window in range(SLOTS):
        start = COLS * window
        if window < SLOTS - 1:
            part = packed[start : start + 2 * COLS]
        else:
            part = jnp.concatenate([packed[start:], packed[:COLS]], axis=0)
        part = part.astype(BF16)
        for group in range(3):
            o_ref[window, 16 * group : 16 * group + 16, :] = part[:, 128 * group : 128 * group + 128]


def pack(levels, x):
    return pl.pallas_call(
        pack_kernel,
        out_shape=jax.ShapeDtypeStruct((SLOTS, PIECE, 128), BF16),
        in_specs=[pl.BlockSpec(memory_space=pltpu.HBM)] * 2,
        out_specs=pl.BlockSpec(memory_space=VMEM),
        scratch_shapes=[
            pltpu.SMEM((SLOTS + 1,), jnp.int32),
            VMEM((C * ROWS, 128), F32),
            pltpu.SemaphoreType.DMA((2,)),
        ],
        name="pack",
        compiler_params=pltpu.CompilerParams(vmem_limit_bytes=12 << 20),
    )(levels, x)


def tables_kernel(levels_hbm, in_w_hbm, bias_hbm, cond_hbm, out_w_hbm, conv_hbm, film_ref, coef_ref, in_pack_ref, in_t_ref, out_t_ref, bias_ref, conv_ref, swap_ref, before_ref, gather_ref, levels_ref, in_w_ref, cond_ref, out_w_ref, sems):
    sources = (levels_hbm, in_w_hbm, cond_hbm, out_w_hbm, bias_hbm, conv_hbm)
    targets = (levels_ref, in_w_ref, cond_ref, out_w_ref, bias_ref, conv_ref)
    copies = [pltpu.make_async_copy(a, b, sems.at[i]) for i, (a, b) in enumerate(zip(sources, targets))]
    for copy in copies:
        copy.start()
    to, frm = iota((256, 256), 0), iota((256, 256), 1)
    swap_ref[...] = one_hot(((to >> 4) == (frm & 15)) & ((to & 15) == (frm >> 4)))
    to, frm = iota((128, 256), 0), iota((128, 256), 1) & 127
    before_ref[...] = one_hot(((to >> 4) == (frm >> 4)) & ((frm & 15) < (to & 15)))
    gather_ref[...] = one_hot(((to & 7) == (frm >> 4)) & ((frm & 15) <= (to >> 3)))
    copies[0].wait()
    place = iota((SLOTS, 128), 0)
    now = jnp.zeros((SLOTS, 128), jnp.int32)
    following = now
    for k in range(SLOTS):
        now = jnp.where(place == k, levels_ref[k], now)
        following = jnp.where(place == k, levels_ref[k + 1], following)
    now, following = sigma_of(now), sigma_of(following)
    variance = now * now + 0.25
    root = jnp.sqrt(variance)
    ratio = (following - now) / now
    coef_ref[0] = 1.0 / root
    coef_ref[1] = root
    coef_ref[2] = (1.0 - 0.25 / variance) * ratio
    coef_ref[3] = 0.5 * now / root * ratio
    j = iota((SLOTS, 128), 1).astype(F32)
    frequency = jnp.exp(j * (jnp.log(F32(100.0)) / 128.0))
    phases = jnp.log(now) / 4.0 * frequency
    embedding = jnp.concatenate([jnp.cos(phases), jnp.sin(phases)], axis=1).astype(BF16)
    copies[1].wait()
    copies[2].wait()
    copies[3].wait()
    conditions = jnp.dot(embedding, cond_ref[...], preferred_element_type=F32)
    film_ref[0] = 0.5 * (1.0 + conditions[:, 0:256])
    film_ref[1] = 0.5 * conditions[:, 256:512]
    film_ref[2] = 0.5 * (1.0 + conditions[:, 512:768])
    film_ref[3] = 0.5 * conditions[:, 768:1024]
    channel, lane = iota((C, 256), 0), iota((C, 256), 1)
    for row in range(ROWS):
        pick = one_hot(lane == lane_of(channel, row))
        in_pack_ref[row] = lax.dot_general(pick, in_w_ref[...], TN, preferred_element_type=F32).astype(BF16)
    eye = one_hot(iota((C, 128), 0) == iota((C, 128), 1))
    in_t_ref[...] = lax.dot_general(eye, in_w_ref[...], TN, preferred_element_type=F32).astype(BF16)
    out_t_ref[...] = lax.dot_general(out_w_ref[...], eye, TN, preferred_element_type=F32).astype(BF16)
    copies[4].wait()
    copies[5].wait()


def tables(levels, in_weight_t, in_bias, cond_weight, out_weight, conv_weight):
    return pl.pallas_call(
        tables_kernel,
        out_shape=[
            jax.ShapeDtypeStruct((4, SLOTS, HID), F32),
            jax.ShapeDtypeStruct((4, SLOTS, 128), F32),
            jax.ShapeDtypeStruct((ROWS, 256, HID), BF16),
            jax.ShapeDtypeStruct((128, HID), BF16),
            jax.ShapeDtypeStruct((HID, 128), BF16),
            jax.ShapeDtypeStruct((1, HID), F32),
            jax.ShapeDtypeStruct((2, HID, 9 * HID), BF16),
            jax.ShapeDtypeStruct((256, 256), BF16),
            jax.ShapeDtypeStruct((128, 256), BF16),
            jax.ShapeDtypeStruct((128, 256), BF16),
        ],
        in_specs=[pl.BlockSpec(memory_space=pltpu.HBM)] * 6,
        out_specs=[pl.BlockSpec(memory_space=VMEM)] * 10,
        scratch_shapes=[
            pltpu.SMEM((SLOTS + 1,), jnp.int32),
            VMEM((C, HID), BF16),
            VMEM((256, 1024), BF16),
            VMEM((C, HID), BF16),
            pltpu.SemaphoreType.DMA((6,)),
        ],
        name="tables",
        compiler_params=pltpu.CompilerParams(vmem_limit_bytes=12 << 20),
    )(levels, in_weight_t, in_bias, cond_weight, out_weight, conv_weight)


def split(value):
    high = value.astype(BF16)
    return high, (value - high.astype(F32)).astype(BF16)


def convolve(ref, top, rows, cells, weight):
    parts = []
    for a in range(3):
        for b in range(3):
            view = ref[top + a : top + a + rows, 16 * b : 16 * b + cells, :]
            parts.append(view.reshape(rows * cells, HID))
    return lax.dot_general(jnp.concatenate(parts, axis=1), weight, NT, preferred_element_type=F32)


def film(response, scale, shift):
    cells = response.shape[0] // SLOTS
    half = response.reshape(cells, SLOTS, HID) * scale[None] + shift[None]
    return (half * jnp.tanh(half) + half).reshape(cells * SLOTS, HID)


def halves(value):
    high, low = split(value)
    return jnp.concatenate([high, low], axis=0)


def main_kernel(low_ref, own_ref, high_ref, film_ref, coef_ref, in_pack_ref, in_t_ref, out_t_ref, bias_ref, conv_ref, swap_ref, before_ref, gather_ref, o_ref, h0, h1, g0, g1, x1, s2):
    place = lax.axis_index("lat")
    count = lax.axis_size("lat")
    inside_low = jnp.where(place > 0, 1.0, 0.0).astype(F32)
    inside_high = jnp.where(place < count - 1, 1.0, 0.0).astype(F32)
    gates = (inside_low, F32(1.0), inside_high)
    bias = bias_ref[...]
    lane = iota((1, 128), 1)
    first = iota((1, SLOTS, 128), 1) == 0

    def gate_of(row):
        return inside_low if row < 0 else inside_high if row >= ROWS else F32(1.0)

    blocks = [
        [ref[:, 16 * group : 16 * group + 16, :].reshape(256, 128) for group in range(3)]
        for ref in (low_ref, own_ref, high_ref)
    ]
    swap = swap_ref[...]

    def swapped(left, right):
        both = jnp.dot(swap, jnp.concatenate([left, right], axis=1), preferred_element_type=F32)
        return both[:, :128], both[:, 128:]

    heads = [swapped(block[0], block[1]) for block in blocks]
    tails = [*swapped(blocks[0][2], blocks[1][2])]
    tails.append(jnp.dot(swap, blocks[2][2], preferred_element_type=F32))

    for row in range(ROWS):
        lhs = jnp.concatenate(
            [jnp.concatenate([heads[at][row & 1], tails[at]], axis=1).astype(BF16) for at in range(3)], axis=0
        )
        hidden = jnp.dot(lhs, in_pack_ref[row], preferred_element_type=F32)
        for at in range(3):
            i = 4 * at + row
            h0[i] = (hidden[256 * at : 256 * at + 256] + bias * gates[at]).astype(BF16)
            if 2 <= i < 10:
                head, tail = heads[at][row & 1][32:224], tails[at][32:224]
                if row >= 2:
                    head = pltpu.roll(head, 64, 1)
                if row != 2:
                    tail = pltpu.roll(tail, (64 - 32 * row) % 128, 1)
                value = jnp.where(lane < 64, head, jnp.where(lane < C, tail, 0.0))
                x1[i - 2] = (value.reshape(12, SLOTS, 128) * coef_ref[1][None]).reshape(192, 128)

    for top in (0, 5):
        response = convolve(h0, top, 5, 224, conv_ref[0])
        for at in range(5):
            gate = gate_of(top + at - 3)
            hidden = film(response[224 * at : 224 * at + 224], film_ref[0] * gate, film_ref[1] * gate)
            h1[top + at] = hidden.astype(BF16)

    for top in (0, 4):
        response = convolve(h1, top, 4, 192, conv_ref[1])
        hidden = h1[top + 1 : top + 5, 16:208, :].reshape(768, HID).astype(F32)
        hidden = hidden + film(response, film_ref[2], film_ref[3])
        network = jnp.dot(hidden.astype(BF16), out_t_ref[...], preferred_element_type=F32)
        x = x1[top : top + 4].reshape(48, SLOTS, 128)
        anchor = jnp.where(first, x, 0.0)
        drift = coef_ref[2][None] * x - coef_ref[3][None] * network.reshape(48, SLOTS, 128) + anchor
        drift = drift.reshape(768, 128)
        earlier = []
        for pair in range(3):
            rhs = [halves(drift[256 * pair + 128 * k : 256 * pair + 128 * k + 128]) for k in range(2)]
            both = jnp.dot(before_ref[...], jnp.concatenate(rhs, axis=1), preferred_element_type=F32)
            earlier += [both[:, :128], both[:, 128:]]
        state = jnp.concatenate(earlier, axis=0).reshape(48, SLOTS, 128) + anchor
        scaled = []
        for at in range(4):
            i = top + at
            here = state[12 * at : 12 * at + 12]
            if 2 <= i < 6:
                s2[i - 2] = here[2:10].reshape(128, 128)
            scaled.append((here * (coef_ref[0] * gate_of(i - 2))[None]).reshape(192, 128).astype(BF16))
        hidden = jnp.dot(jnp.concatenate(scaled, axis=0), in_t_ref[...], preferred_element_type=F32)
        for at in range(4):
            g0[top + at] = (hidden[192 * at : 192 * at + 192] + bias * gate_of(top + at - 2)).astype(BF16)

    for top in (0, 3):
        response = convolve(g0, top, 3, 160, conv_ref[0])
        for at in range(3):
            gate = gate_of(top + at - 1)
            hidden = film(response[160 * at : 160 * at + 160], film_ref[0] * gate, film_ref[1] * gate)
            g1[top + at] = hidden.astype(BF16)

    response = convolve(g1, 0, 4, 128, conv_ref[1])
    hidden = g1[1:5, 16:144, :].reshape(512, HID).astype(F32)
    hidden = hidden + film(response, film_ref[2], film_ref[3])
    network = jnp.dot(hidden.astype(BF16), out_t_ref[...], preferred_element_type=F32)
    state = s2[...].reshape(32, SLOTS, 128)
    anchor = jnp.where(first, state, 0.0)
    drift = coef_ref[2][None] * state - coef_ref[3][None] * network.reshape(32, SLOTS, 128) + anchor
    drift = drift.reshape(512, 128)
    done = []
    for pair in range(2):
        rhs = [halves(drift[256 * pair + 128 * k : 256 * pair + 128 * k + 128]) for k in range(2)]
        both = jnp.dot(gather_ref[...], jnp.concatenate(rhs, axis=1), preferred_element_type=F32)
        done += [both[:, :128], both[:, 128:]]
    tail = pltpu.roll(done[0], 64, 1)
    for row in range(1, ROWS):
        here = done[row] if row == 2 else pltpu.roll(done[row], (32 * row - 64) % 128, 1)
        tail = jnp.where(lane < 32 * row, tail, here)
    for half in range(2):
        head = jnp.where(lane < 64, done[half], pltpu.roll(done[half + 2], 64, 1))
        o_ref[:, COLS * half : COLS * half + COLS, :] = head.reshape(SLOTS, COLS, 128).astype(BF16)
    o_ref[:, 2 * COLS :, :] = tail.reshape(SLOTS, COLS, 128).astype(BF16)


def main(low, own, high, prepared):
    return pl.pallas_call(
        main_kernel,
        out_shape=jax.ShapeDtypeStruct((SLOTS, BACK, 128), BF16),
        in_specs=[pl.BlockSpec(memory_space=VMEM)] * 13,
        out_specs=pl.BlockSpec(memory_space=VMEM),
        scratch_shapes=[
            VMEM((12, 256, HID), BF16),
            VMEM((10, 224, HID), BF16),
            VMEM((8, 192, HID), BF16),
            VMEM((6, 160, HID), BF16),
            VMEM((8, 192, 128), F32),
            VMEM((ROWS, 128, 128), F32),
        ],
        name="patch",
        compiler_params=pltpu.CompilerParams(vmem_limit_bytes=32 << 20),
    )(low, own, high, *prepared)


def unpack_kernel(p_ref, o_ref):
    pieces = p_ref[...].astype(F32)

    def turned(group):
        return pieces[:, COLS * group : COLS * group + COLS, :].reshape(128, 128).T

    heads, tail = [turned(0), turned(1)], turned(2)
    for row in range(ROWS):
        start = 64 if row >= 2 else 0
        o_ref[pl.ds(row, 64, stride=ROWS), :] = heads[row & 1][start : start + 64]
        o_ref[pl.ds(64 * ROWS + row, C - 64, stride=ROWS), :] = tail[32 * row : 32 * row + C - 64]


def unpack(pieces):
    return pl.pallas_call(
        unpack_kernel,
        out_shape=jax.ShapeDtypeStruct((C * ROWS, 128), F32),
        in_specs=[pl.BlockSpec(memory_space=VMEM)],
        out_specs=pl.BlockSpec(memory_space=VMEM),
        name="unpack",
        compiler_params=pltpu.CompilerParams(vmem_limit_bytes=8 << 20),
    )(pieces)


def on_device(trajectory, step_levels, in_weight, in_bias, conv_weight, cond_weight, out_weight):
    count = lax.axis_size("lat")
    forward = [(i, i + 1) for i in range(count - 1)]
    backward = [(b, a) for a, b in forward]
    pieces = pack(step_levels, trajectory.reshape(C * ROWS, 128))
    own = lax.all_to_all(pieces, "tm", 0, 0)
    prepared = tables(step_levels, in_weight.T, in_bias[None, :], cond_weight, out_weight, conv_weight)
    own, prepared = lax.optimization_barrier((own, prepared))
    low = lax.ppermute(own, "lat", forward)
    high = lax.ppermute(own, "lat", backward)
    done = main(low, own, high, prepared)
    back = lax.all_to_all(done, "tm", 0, 0)
    return unpack(back).reshape(1, C, ROWS, 128)


def solution(mesh):
    in_specs = (P("tm", None, "lat", None), P(), P(), P(), P(), P(), P())
    out_specs = P("tm", None, "lat", None)
    return jax.shard_map(on_device, mesh=mesh, in_specs=in_specs, out_specs=out_specs, check_vma=False)
```

```python
import functools

import jax
import jax.numpy as jnp
from jax import lax
from jax.experimental import pallas as pl
from jax.experimental.pallas import tpu as pltpu
from jax.sharding import PartitionSpec as P

LEVELS = 64
C = 84
HID = 256
SLOTS = 16
ROWS = 4
COLS = 8
PIECE = 48
BACK = 24

SIGMA_TOP = 1.0
SIGMA_LOW = 0.02
RHO = 7.0
ROOT_TOP = SIGMA_TOP ** (1.0 / RHO)
ROOT_LOW = SIGMA_LOW ** (1.0 / RHO)

F32 = jnp.float32
BF16 = jnp.bfloat16
VMEM = pltpu.VMEM
NT = (((1,), (1,)), ((), ()))
TN = (((0,), (0,)), ((), ()))


def iota(shape, dim):
    return lax.broadcasted_iota(jnp.int32, shape, dim)


def one_hot(mask):
    return jnp.where(mask, 1.0, 0.0).astype(BF16)


def sigma_of(level):
    root = ROOT_TOP + level.astype(F32) / (LEVELS - 1) * (ROOT_LOW - ROOT_TOP)
    square = root * root
    return square * square * square * root


def lane_of(channel, row):
    head = channel + jnp.where(row >= 2, 64, 0)
    tail = 128 + 32 * row + (channel - 64)
    return jnp.where(channel < 64, head, tail)


def pack_kernel(levels_hbm, x_hbm, o_ref, levels_ref, x_ref, sems):
    get_levels = pltpu.make_async_copy(levels_hbm, levels_ref, sems.at[0])
    get_x = pltpu.make_async_copy(x_hbm, x_ref, sems.at[1])
    get_levels.start()
    get_x.start()
    slot = lax.axis_index("tm")
    shape = (C * ROWS, 3 * 128)
    index, lane = iota(shape, 0), iota(shape, 1)
    channel, row = index >> 2, index & 3
    target = lane_of(channel, row)
    target = jnp.where(target < 128, target + 128 * (row & 1), target + 128)
    places = one_hot(lane == target)
    get_levels.wait()
    sigma = sigma_of(jnp.full((1, 128), levels_ref[slot], jnp.int32))
    scale = jnp.sqrt(sigma * sigma + 0.25)
    get_x.wait()
    scaled = pltpu.roll(x_ref[...] / scale, 4, 1).astype(BF16)
    packed = lax.dot_general(scaled, places, TN, preferred_element_type=F32)
    for window in range(SLOTS):
        start = COLS * window
        if window < SLOTS - 1:
            part = packed[start : start + 2 * COLS]
        else:
            part = jnp.concatenate([packed[start:], packed[:COLS]], axis=0)
        part = part.astype(BF16)
        for group in range(3):
            o_ref[window, 16 * group : 16 * group + 16, :] = part[:, 128 * group : 128 * group + 128]


def pack(levels, x):
    return pl.pallas_call(
        pack_kernel,
        out_shape=jax.ShapeDtypeStruct((SLOTS, PIECE, 128), BF16),
        in_specs=[pl.BlockSpec(memory_space=pltpu.HBM)] * 2,
        out_specs=pl.BlockSpec(memory_space=VMEM),
        scratch_shapes=[
            pltpu.SMEM((SLOTS + 1,), jnp.int32),
            VMEM((C * ROWS, 128), F32),
            pltpu.SemaphoreType.DMA((2,)),
        ],
        name="pack",
        compiler_params=pltpu.CompilerParams(vmem_limit_bytes=60 * 1024 * 1024),
    )(levels, x)


def tables_kernel(levels_hbm, in_w_hbm, bias_hbm, cond_hbm, out_w_hbm, conv_hbm, film_ref, in_pack_ref, in_t_ref, out_t_ref, bias_ref, conv_ref, swap_ref, before_ref, gather_ref, levels_ref, in_w_ref, cond_ref, out_w_ref, sems):
    sources = (levels_hbm, in_w_hbm, cond_hbm, out_w_hbm, bias_hbm, conv_hbm)
    targets = (levels_ref, in_w_ref, cond_ref, out_w_ref, bias_ref, conv_ref)
    copies = [pltpu.make_async_copy(a, b, sems.at[i]) for i, (a, b) in enumerate(zip(sources, targets))]
    for copy in copies:
        copy.start()
    to, frm = iota((256, 256), 0), iota((256, 256), 1)
    swap_ref[...] = one_hot(((to >> 4) == (frm & 15)) & ((to & 15) == (frm >> 4)))
    to, frm = iota((128, 256), 0), iota((128, 256), 1) & 127
    before_ref[...] = one_hot(((to >> 4) == (frm >> 4)) & ((frm & 15) < (to & 15)))
    gather_ref[...] = one_hot(((to & 7) == (frm >> 4)) & ((frm & 15) <= (to >> 3)))
    copies[0].wait()
    place = iota((SLOTS, 128), 0)
    now = jnp.zeros((SLOTS, 128), jnp.int32)
    following = now
    for k in range(SLOTS):
        now = jnp.where(place == k, levels_ref[k], now)
        following = jnp.where(place == k, levels_ref[k + 1], following)
    now, following = sigma_of(now), sigma_of(following)
    variance = now * now + 0.25
    root = jnp.sqrt(variance)
    ratio = (following - now) / now
    film_ref[4, :, :128] = 1.0 / root
    film_ref[4, :, 128:] = root
    film_ref[5, :, :128] = (1.0 - 0.25 / variance) * ratio
    film_ref[5, :, 128:] = 0.5 * now / root * ratio
    j = iota((SLOTS, 128), 1).astype(F32)
    frequency = jnp.exp(j * (jnp.log(F32(100.0)) / 128.0))
    phases = jnp.log(now) / 4.0 * frequency
    embedding = jnp.concatenate([jnp.cos(phases), jnp.sin(phases)], axis=1).astype(BF16)
    copies[1].wait()
    copies[2].wait()
    copies[3].wait()
    conditions = jnp.dot(embedding, cond_ref[...], preferred_element_type=F32)
    film_ref[0] = 0.5 * (1.0 + conditions[:, 0:256])
    film_ref[1] = 0.5 * conditions[:, 256:512]
    film_ref[2] = 0.5 * (1.0 + conditions[:, 512:768])
    film_ref[3] = 0.5 * conditions[:, 768:1024]
    channel, lane = iota((C, 256), 0), iota((C, 256), 1)
    for row in range(ROWS):
        pick = one_hot(lane == lane_of(channel, row))
        in_pack_ref[row] = lax.dot_general(pick, in_w_ref[...], TN, preferred_element_type=F32).astype(BF16)
    eye = one_hot(iota((C, 128), 0) == iota((C, 128), 1))
    in_t_ref[...] = lax.dot_general(eye, in_w_ref[...], TN, preferred_element_type=F32).astype(BF16)
    out_t_ref[...] = lax.dot_general(out_w_ref[...], eye, TN, preferred_element_type=F32).astype(BF16)
    copies[4].wait()
    copies[5].wait()


def tables(levels, in_weight_t, in_bias, cond_weight, out_weight, conv_weight):
    return pl.pallas_call(
        tables_kernel,
        out_shape=[
            jax.ShapeDtypeStruct((6, SLOTS, HID), F32),
            jax.ShapeDtypeStruct((ROWS, 256, HID), BF16),
            jax.ShapeDtypeStruct((128, HID), BF16),
            jax.ShapeDtypeStruct((HID, 128), BF16),
            jax.ShapeDtypeStruct((1, HID), F32),
            jax.ShapeDtypeStruct((2, HID, 9 * HID), BF16),
            jax.ShapeDtypeStruct((256, 256), BF16),
            jax.ShapeDtypeStruct((128, 256), BF16),
            jax.ShapeDtypeStruct((128, 256), BF16),
        ],
        in_specs=[pl.BlockSpec(memory_space=pltpu.HBM)] * 6,
        out_specs=[pl.BlockSpec(memory_space=VMEM)] * 9,
        scratch_shapes=[
            pltpu.SMEM((SLOTS + 1,), jnp.int32),
            VMEM((C, HID), BF16),
            VMEM((256, 1024), BF16),
            VMEM((C, HID), BF16),
            pltpu.SemaphoreType.DMA((6,)),
        ],
        name="tables",
        compiler_params=pltpu.CompilerParams(vmem_limit_bytes=61400 << 10),
    )(levels, in_weight_t, in_bias, cond_weight, out_weight, conv_weight)


def split(value):
    high = value.astype(BF16)
    return high, (value - high.astype(F32)).astype(BF16)


def convolve(ref, top, rows, cells, weight):
    parts = []
    for a in range(3):
        for b in range(3):
            view = ref[top + a : top + a + rows, 16 * b : 16 * b + cells, :]
            parts.append(view.reshape(rows * cells, HID))
    return lax.dot_general(jnp.concatenate(parts, axis=1), weight, NT, preferred_element_type=F32)


def film(response, scale, shift):
    cells = response.shape[0] // SLOTS
    half = response.reshape(cells, SLOTS, HID) * scale[None] + shift[None]
    return (half * jnp.tanh(half) + half).reshape(cells * SLOTS, HID)


def halves(value):
    high, low = split(value)
    return jnp.concatenate([high, low], axis=0)


def main_kernel(low_ref, own_ref, high_ref, film_ref, in_pack_ref, in_t_ref, out_t_ref, bias_ref, conv_ref, swap_ref, before_ref, gather_ref, o_ref, h0, h1, g0, g1, x1, s2):
    place = lax.axis_index("lat")
    count = lax.axis_size("lat")
    inside_low = jnp.where(place > 0, 1.0, 0.0).astype(F32)
    inside_high = jnp.where(place < count - 1, 1.0, 0.0).astype(F32)
    gates = (inside_low, F32(1.0), inside_high)
    bias = bias_ref[...]
    lane = iota((1, 128), 1)
    first = iota((1, SLOTS, 128), 1) == 0

    def gate_of(row):
        return inside_low if row < 0 else inside_high if row >= ROWS else F32(1.0)

    blocks = [
        [ref[:, 16 * group : 16 * group + 16, :].reshape(256, 128) for group in range(3)]
        for ref in (low_ref, own_ref, high_ref)
    ]
    swap = swap_ref[...]

    def swapped(left, right):
        both = jnp.dot(swap, jnp.concatenate([left, right], axis=1), preferred_element_type=F32)
        return both[:, :128], both[:, 128:]

    heads = [swapped(block[0], block[1]) for block in blocks]
    tails = [*swapped(blocks[0][2], blocks[1][2])]
    tails.append(jnp.dot(swap, blocks[2][2], preferred_element_type=F32))

    for row in range(ROWS):
        lhs = jnp.concatenate(
            [jnp.concatenate([heads[at][row & 1], tails[at]], axis=1).astype(BF16) for at in range(3)], axis=0
        )
        hidden = jnp.dot(lhs, in_pack_ref[row], preferred_element_type=F32)
        for at in range(3):
            i = 4 * at + row
            h0[i] = (hidden[256 * at : 256 * at + 256] + bias * gates[at]).astype(BF16)
            if 2 <= i < 10:
                head, tail = heads[at][row & 1][32:224], tails[at][32:224]
                if row >= 2:
                    head = pltpu.roll(head, 64, 1)
                if row != 2:
                    tail = pltpu.roll(tail, (64 - 32 * row) % 128, 1)
                value = jnp.where(lane < 64, head, jnp.where(lane < C, tail, 0.0))
                x1[i - 2] = (value.reshape(12, SLOTS, 128) * film_ref[4, :, 128:][None]).reshape(192, 128)

    for top in (0, 5):
        response = convolve(h0, top, 5, 224, conv_ref[0])
        for at in range(5):
            gate = gate_of(top + at - 3)
            hidden = film(response[224 * at : 224 * at + 224], film_ref[0] * gate, film_ref[1] * gate)
            h1[top + at] = hidden.astype(BF16)

    for top in (0, 4):
        response = convolve(h1, top, 4, 192, conv_ref[1])
        hidden = h1[top + 1 : top + 5, 16:208, :].reshape(768, HID).astype(F32)
        hidden = hidden + film(response, film_ref[2], film_ref[3])
        network = jnp.dot(hidden.astype(BF16), out_t_ref[...], preferred_element_type=F32)
        x = x1[top : top + 4].reshape(48, SLOTS, 128)
        anchor = jnp.where(first, x, 0.0)
        drift = film_ref[5, :, :128][None] * x - film_ref[5, :, 128:][None] * network.reshape(48, SLOTS, 128) + anchor
        drift = drift.reshape(768, 128)
        earlier = []
        for pair in range(3):
            rhs = [halves(drift[256 * pair + 128 * k : 256 * pair + 128 * k + 128]) for k in range(2)]
            both = jnp.dot(before_ref[...], jnp.concatenate(rhs, axis=1), preferred_element_type=F32)
            earlier += [both[:, :128], both[:, 128:]]
        state = jnp.concatenate(earlier, axis=0).reshape(48, SLOTS, 128) + anchor
        scaled = []
        for at in range(4):
            i = top + at
            here = state[12 * at : 12 * at + 12]
            if 2 <= i < 6:
                s2[i - 2] = here[2:10].reshape(128, 128)
            scaled.append((here * (film_ref[4, :, :128] * gate_of(i - 2))[None]).reshape(192, 128).astype(BF16))
        hidden = jnp.dot(jnp.concatenate(scaled, axis=0), in_t_ref[...], preferred_element_type=F32)
        for at in range(4):
            g0[top + at] = (hidden[192 * at : 192 * at + 192] + bias * gate_of(top + at - 2)).astype(BF16)

    for top in (0, 3):
        response = convolve(g0, top, 3, 160, conv_ref[0])
        for at in range(3):
            gate = gate_of(top + at - 1)
            hidden = film(response[160 * at : 160 * at + 160], film_ref[0] * gate, film_ref[1] * gate)
            g1[top + at] = hidden.astype(BF16)

    response = convolve(g1, 0, 4, 128, conv_ref[1])
    hidden = g1[1:5, 16:144, :].reshape(512, HID).astype(F32)
    hidden = hidden + film(response, film_ref[2], film_ref[3])
    network = jnp.dot(hidden.astype(BF16), out_t_ref[...], preferred_element_type=F32)
    state = s2[...].reshape(32, SLOTS, 128)
    anchor = jnp.where(first, state, 0.0)
    drift = film_ref[5, :, :128][None] * state - film_ref[5, :, 128:][None] * network.reshape(32, SLOTS, 128) + anchor
    drift = drift.reshape(512, 128)
    done = []
    for pair in range(2):
        rhs = [halves(drift[256 * pair + 128 * k : 256 * pair + 128 * k + 128]) for k in range(2)]
        both = jnp.dot(gather_ref[...], jnp.concatenate(rhs, axis=1), preferred_element_type=F32)
        done += [both[:, :128], both[:, 128:]]
    tail = pltpu.roll(done[0], 64, 1)
    for row in range(1, ROWS):
        here = done[row] if row == 2 else pltpu.roll(done[row], (32 * row - 64) % 128, 1)
        tail = jnp.where(lane < 32 * row, tail, here)
    for half in range(2):
        head = jnp.where(lane < 64, done[half], pltpu.roll(done[half + 2], 64, 1))
        o_ref[:, COLS * half : COLS * half + COLS, :] = head.reshape(SLOTS, COLS, 128).astype(BF16)
    o_ref[:, 2 * COLS :, :] = tail.reshape(SLOTS, COLS, 128).astype(BF16)


def main(low, own, high, prepared):
    return pl.pallas_call(
        main_kernel,
        out_shape=jax.ShapeDtypeStruct((SLOTS, BACK, 128), BF16),
        in_specs=[pl.BlockSpec(memory_space=VMEM)] * 12,
        out_specs=pl.BlockSpec(memory_space=VMEM),
        scratch_shapes=[
            VMEM((12, 256, HID), BF16),
            VMEM((10, 224, HID), BF16),
            VMEM((8, 192, HID), BF16),
            VMEM((6, 160, HID), BF16),
            VMEM((8, 192, 128), F32),
            VMEM((ROWS, 128, 128), F32),
        ],
        name="patch",
        compiler_params=pltpu.CompilerParams(vmem_limit_bytes=32 << 20),
    )(low, own, high, *prepared)


def unpack_kernel(p_ref, o_ref):
    pieces = p_ref[...].astype(F32)

    def turned(group):
        return pieces[:, COLS * group : COLS * group + COLS, :].reshape(128, 128).T

    heads, tail = [turned(0), turned(1)], turned(2)
    for row in range(ROWS):
        start = 64 if row >= 2 else 0
        o_ref[pl.ds(row, 64, stride=ROWS), :] = heads[row & 1][start : start + 64]
        o_ref[pl.ds(64 * ROWS + row, C - 64, stride=ROWS), :] = tail[32 * row : 32 * row + C - 64]


def unpack(pieces):
    return pl.pallas_call(
        unpack_kernel,
        out_shape=jax.ShapeDtypeStruct((C * ROWS, 128), F32),
        in_specs=[pl.BlockSpec(memory_space=VMEM)],
        out_specs=pl.BlockSpec(memory_space=VMEM),
        name="unpack",
        compiler_params=pltpu.CompilerParams(vmem_limit_bytes=8 << 20),
    )(pieces)


def on_device(trajectory, step_levels, in_weight, in_bias, conv_weight, cond_weight, out_weight):
    count = lax.axis_size("lat")
    forward = [(i, i + 1) for i in range(count - 1)]
    backward = [(b, a) for a, b in forward]
    pieces = pack(step_levels, trajectory.reshape(C * ROWS, 128))
    own = lax.all_to_all(pieces, "tm", 0, 0)
    prepared = tables(step_levels, in_weight.T, in_bias[None, :], cond_weight, out_weight, conv_weight)
    own, prepared = lax.optimization_barrier((own, prepared))
    low = lax.ppermute(own, "lat", forward)
    high = lax.ppermute(own, "lat", backward)
    done = main(low, own, high, prepared)
    back = lax.all_to_all(done, "tm", 0, 0)
    return unpack(back).reshape(1, C, ROWS, 128)


def solution(mesh):
    in_specs = (P("tm", None, "lat", None), P(), P(), P(), P(), P(), P())
    out_specs = P("tm", None, "lat", None)
    return jax.shard_map(on_device, mesh=mesh, in_specs=in_specs, out_specs=out_specs, check_vma=False)
```

```python
import functools

import jax
import jax.numpy as jnp
from jax import lax
from jax.experimental import pallas as pl
from jax.experimental.pallas import tpu as pltpu
from jax.sharding import PartitionSpec as P

LEVELS = 64
C = 84
HID = 256
SLOTS = 16
ROWS = 4
COLS = 8
PIECE = 48
BACK = 24

SIGMA_TOP = 1.0
SIGMA_LOW = 0.02
RHO = 7.0
ROOT_TOP = SIGMA_TOP ** (1.0 / RHO)
ROOT_LOW = SIGMA_LOW ** (1.0 / RHO)

F32 = jnp.float32
BF16 = jnp.bfloat16
VMEM = pltpu.VMEM
NT = (((1,), (1,)), ((), ()))
TN = (((0,), (0,)), ((), ()))


def iota(shape, dim):
    return lax.broadcasted_iota(jnp.int32, shape, dim)


def one_hot(mask):
    return jnp.where(mask, 1.0, 0.0).astype(BF16)


def sigma_of(level):
    root = ROOT_TOP + level.astype(F32) / (LEVELS - 1) * (ROOT_LOW - ROOT_TOP)
    square = root * root
    return square * square * square * root


def lane_of(channel, row):
    head = channel + jnp.where(row >= 2, 64, 0)
    tail = 128 + 32 * row + (channel - 64)
    return jnp.where(channel < 64, head, tail)


def pack_kernel(levels_hbm, x_hbm, o_ref, levels_ref, x_ref, sems):
    get_levels = pltpu.make_async_copy(levels_hbm, levels_ref, sems.at[0])
    get_x = pltpu.make_async_copy(x_hbm, x_ref, sems.at[1])
    get_levels.start()
    get_x.start()
    slot = lax.axis_index("tm")
    shape = (C * ROWS, 3 * 128)
    index, lane = iota(shape, 0), iota(shape, 1)
    channel, row = index >> 2, index & 3
    target = lane_of(channel, row)
    target = jnp.where(target < 128, target + 128 * (row & 1), target + 128)
    places = one_hot(lane == target)
    get_levels.wait()
    sigma = sigma_of(jnp.full((1, 128), levels_ref[slot], jnp.int32))
    scale = jnp.sqrt(sigma * sigma + 0.25)
    get_x.wait()
    scaled = pltpu.roll(x_ref[...] / scale, 4, 1).astype(BF16)
    packed = lax.dot_general(scaled, places, TN, preferred_element_type=F32)
    for window in range(SLOTS):
        start = COLS * window
        if window < SLOTS - 1:
            part = packed[start : start + 2 * COLS]
        else:
            part = jnp.concatenate([packed[start:], packed[:COLS]], axis=0)
        part = part.astype(BF16)
        for group in range(3):
            o_ref[window, 16 * group : 16 * group + 16, :] = part[:, 128 * group : 128 * group + 128]


def pack(levels, x):
    return pl.pallas_call(
        pack_kernel,
        out_shape=jax.ShapeDtypeStruct((SLOTS, PIECE, 128), BF16),
        in_specs=[pl.BlockSpec(memory_space=pltpu.HBM)] * 2,
        out_specs=pl.BlockSpec(memory_space=VMEM),
        scratch_shapes=[
            pltpu.SMEM((SLOTS + 1,), jnp.int32),
            VMEM((C * ROWS, 128), F32),
            pltpu.SemaphoreType.DMA((2,)),
        ],
        name="pack",
        compiler_params=pltpu.CompilerParams(vmem_limit_bytes=12000 << 10),
    )(*[pltpu.with_memory_space_constraint(v, pltpu.HBM) for v in (levels, x)])


def tables_kernel(levels_hbm, in_w_hbm, bias_hbm, cond_hbm, out_w_hbm, conv_hbm, film_ref, in_pack_ref, in_t_ref, out_t_ref, bias_ref, conv_ref, swap_ref, before_ref, gather_ref, levels_ref, in_w_ref, cond_ref, out_w_ref, sems):
    sources = (levels_hbm, in_w_hbm, cond_hbm, out_w_hbm, bias_hbm, conv_hbm)
    targets = (levels_ref, in_w_ref, cond_ref, out_w_ref, bias_ref, conv_ref)
    copies = [pltpu.make_async_copy(a, b, sems.at[i]) for i, (a, b) in enumerate(zip(sources, targets))]
    for copy in copies:
        copy.start()
    to, frm = iota((256, 256), 0), iota((256, 256), 1)
    swap_ref[...] = one_hot(((to >> 4) == (frm & 15)) & ((to & 15) == (frm >> 4)))
    to, frm = iota((128, 256), 0), iota((128, 256), 1) & 127
    before_ref[...] = one_hot(((to >> 4) == (frm >> 4)) & ((frm & 15) < (to & 15)))
    gather_ref[...] = one_hot(((to & 7) == (frm >> 4)) & ((frm & 15) <= (to >> 3)))
    copies[0].wait()
    place = iota((SLOTS, 128), 0)
    now = jnp.zeros((SLOTS, 128), jnp.int32)
    following = now
    for k in range(SLOTS):
        now = jnp.where(place == k, levels_ref[k], now)
        following = jnp.where(place == k, levels_ref[k + 1], following)
    now, following = sigma_of(now), sigma_of(following)
    variance = now * now + 0.25
    root = jnp.sqrt(variance)
    ratio = (following - now) / now
    film_ref[4, :, :128] = 1.0 / root
    film_ref[4, :, 128:] = root
    film_ref[5, :, :128] = (1.0 - 0.25 / variance) * ratio
    film_ref[5, :, 128:] = 0.5 * now / root * ratio
    j = iota((SLOTS, 128), 1).astype(F32)
    frequency = jnp.exp(j * (jnp.log(F32(100.0)) / 128.0))
    phases = jnp.log(now) / 4.0 * frequency
    embedding = jnp.concatenate([jnp.cos(phases), jnp.sin(phases)], axis=1).astype(BF16)
    copies[1].wait()
    copies[2].wait()
    copies[3].wait()
    conditions = jnp.dot(embedding, cond_ref[...], preferred_element_type=F32)
    film_ref[0] = 0.5 * (1.0 + conditions[:, 0:256])
    film_ref[1] = 0.5 * conditions[:, 256:512]
    film_ref[2] = 0.5 * (1.0 + conditions[:, 512:768])
    film_ref[3] = 0.5 * conditions[:, 768:1024]
    channel, lane = iota((C, 256), 0), iota((C, 256), 1)
    for row in range(ROWS):
        pick = one_hot(lane == lane_of(channel, row))
        in_pack_ref[row] = lax.dot_general(pick, in_w_ref[...], TN, preferred_element_type=F32).astype(BF16)
    eye = one_hot(iota((C, 128), 0) == iota((C, 128), 1))
    in_t_ref[...] = lax.dot_general(eye, in_w_ref[...], TN, preferred_element_type=F32).astype(BF16)
    out_t_ref[...] = lax.dot_general(out_w_ref[...], eye, TN, preferred_element_type=F32).astype(BF16)
    copies[4].wait()
    copies[5].wait()


def tables(levels, in_weight_t, in_bias, cond_weight, out_weight, conv_weight):
    return pl.pallas_call(
        tables_kernel,
        out_shape=[
            jax.ShapeDtypeStruct((6, SLOTS, HID), F32),
            jax.ShapeDtypeStruct((ROWS, 256, HID), BF16),
            jax.ShapeDtypeStruct((128, HID), BF16),
            jax.ShapeDtypeStruct((HID, 128), BF16),
            jax.ShapeDtypeStruct((1, HID), F32),
            jax.ShapeDtypeStruct((2, HID, 9 * HID), BF16),
            jax.ShapeDtypeStruct((256, 256), BF16),
            jax.ShapeDtypeStruct((128, 256), BF16),
            jax.ShapeDtypeStruct((128, 256), BF16),
        ],
        in_specs=[pl.BlockSpec(memory_space=pltpu.HBM)] * 6,
        out_specs=[pl.BlockSpec(memory_space=VMEM)] * 9,
        scratch_shapes=[
            pltpu.SMEM((SLOTS + 1,), jnp.int32),
            VMEM((C, HID), BF16),
            VMEM((256, 1024), BF16),
            VMEM((C, HID), BF16),
            pltpu.SemaphoreType.DMA((6,)),
        ],
        name="tables",
        compiler_params=pltpu.CompilerParams(vmem_limit_bytes=12000 << 10),
    )(*[pltpu.with_memory_space_constraint(v, pltpu.HBM) for v in (levels, in_weight_t, in_bias, cond_weight, out_weight, conv_weight)])


def split(value):
    high = value.astype(BF16)
    return high, (value - high.astype(F32)).astype(BF16)


def convolve(ref, top, rows, cells, weight):
    parts = []
    for a in range(3):
        for b in range(3):
            view = ref[top + a : top + a + rows, 16 * b : 16 * b + cells, :]
            parts.append(view.reshape(rows * cells, HID))
    return lax.dot_general(jnp.concatenate(parts, axis=1), weight, NT, preferred_element_type=F32)


def film(response, scale, shift):
    cells = response.shape[0] // SLOTS
    half = response.reshape(cells, SLOTS, HID) * scale[None] + shift[None]
    return (half * jnp.tanh(half) + half).reshape(cells * SLOTS, HID)


def halves(value):
    high, low = split(value)
    return jnp.concatenate([high, low], axis=0)


def main_kernel(low_ref, own_ref, high_ref, film_ref, in_pack_ref, in_t_ref, out_t_ref, bias_ref, conv_ref, swap_ref, before_ref, gather_ref, o_ref, h0, h1, g0, g1, x1, s2):
    place = lax.axis_index("lat")
    count = lax.axis_size("lat")
    inside_low = jnp.where(place > 0, 1.0, 0.0).astype(F32)
    inside_high = jnp.where(place < count - 1, 1.0, 0.0).astype(F32)
    gates = (inside_low, F32(1.0), inside_high)
    bias = bias_ref[...]
    lane = iota((1, 128), 1)
    first = iota((1, SLOTS, 128), 1) == 0

    def gate_of(row):
        return inside_low if row < 0 else inside_high if row >= ROWS else F32(1.0)

    blocks = [
        [ref[:, 16 * group : 16 * group + 16, :].reshape(256, 128) for group in range(3)]
        for ref in (low_ref, own_ref, high_ref)
    ]
    swap = swap_ref[...]

    def swapped(left, right):
        both = jnp.dot(swap, jnp.concatenate([left, right], axis=1), preferred_element_type=F32)
        return both[:, :128], both[:, 128:]

    heads = [swapped(block[0], block[1]) for block in blocks]
    tails = [*swapped(blocks[0][2], blocks[1][2])]
    tails.append(jnp.dot(swap, blocks[2][2], preferred_element_type=F32))

    for row in range(ROWS):
        lhs = jnp.concatenate(
            [jnp.concatenate([heads[at][row & 1], tails[at]], axis=1).astype(BF16) for at in range(3)], axis=0
        )
        hidden = jnp.dot(lhs, in_pack_ref[row], preferred_element_type=F32)
        for at in range(3):
            i = 4 * at + row
            h0[i] = (hidden[256 * at : 256 * at + 256] + bias * gates[at]).astype(BF16)
            if 2 <= i < 10:
                head, tail = heads[at][row & 1][32:224], tails[at][32:224]
                if row >= 2:
                    head = pltpu.roll(head, 64, 1)
                if row != 2:
                    tail = pltpu.roll(tail, (64 - 32 * row) % 128, 1)
                value = jnp.where(lane < 64, head, jnp.where(lane < C, tail, 0.0))
                x1[i - 2] = (value.reshape(12, SLOTS, 128) * film_ref[4, :, 128:][None]).reshape(192, 128)

    for top in (0, 5):
        response = convolve(h0, top, 5, 224, conv_ref[0])
        for at in range(5):
            gate = gate_of(top + at - 3)
            hidden = film(response[224 * at : 224 * at + 224], film_ref[0] * gate, film_ref[1] * gate)
            h1[top + at] = hidden.astype(BF16)

    for top in (0, 4):
        response = convolve(h1, top, 4, 192, conv_ref[1])
        hidden = h1[top + 1 : top + 5, 16:208, :].reshape(768, HID).astype(F32)
        hidden = hidden + film(response, film_ref[2], film_ref[3])
        network = jnp.dot(hidden.astype(BF16), out_t_ref[...], preferred_element_type=F32)
        x = x1[top : top + 4].reshape(48, SLOTS, 128)
        anchor = jnp.where(first, x, 0.0)
        drift = film_ref[5, :, :128][None] * x - film_ref[5, :, 128:][None] * network.reshape(48, SLOTS, 128) + anchor
        drift = drift.reshape(768, 128)
        earlier = []
        for pair in range(3):
            rhs = [halves(drift[256 * pair + 128 * k : 256 * pair + 128 * k + 128]) for k in range(2)]
            both = jnp.dot(before_ref[...], jnp.concatenate(rhs, axis=1), preferred_element_type=F32)
            earlier += [both[:, :128], both[:, 128:]]
        state = jnp.concatenate(earlier, axis=0).reshape(48, SLOTS, 128) + anchor
        scaled = []
        for at in range(4):
            i = top + at
            here = state[12 * at : 12 * at + 12]
            if 2 <= i < 6:
                s2[i - 2] = here[2:10].reshape(128, 128)
            scaled.append((here * (film_ref[4, :, :128] * gate_of(i - 2))[None]).reshape(192, 128).astype(BF16))
        hidden = jnp.dot(jnp.concatenate(scaled, axis=0), in_t_ref[...], preferred_element_type=F32)
        for at in range(4):
            g0[top + at] = (hidden[192 * at : 192 * at + 192] + bias * gate_of(top + at - 2)).astype(BF16)

    for top in (0, 3):
        response = convolve(g0, top, 3, 160, conv_ref[0])
        for at in range(3):
            gate = gate_of(top + at - 1)
            hidden = film(response[160 * at : 160 * at + 160], film_ref[0] * gate, film_ref[1] * gate)
            g1[top + at] = hidden.astype(BF16)

    response = convolve(g1, 0, 4, 128, conv_ref[1])
    hidden = g1[1:5, 16:144, :].reshape(512, HID).astype(F32)
    hidden = hidden + film(response, film_ref[2], film_ref[3])
    network = jnp.dot(hidden.astype(BF16), out_t_ref[...], preferred_element_type=F32)
    state = s2[...].reshape(32, SLOTS, 128)
    anchor = jnp.where(first, state, 0.0)
    drift = film_ref[5, :, :128][None] * state - film_ref[5, :, 128:][None] * network.reshape(32, SLOTS, 128) + anchor
    drift = drift.reshape(512, 128)
    done = []
    for pair in range(2):
        rhs = [halves(drift[256 * pair + 128 * k : 256 * pair + 128 * k + 128]) for k in range(2)]
        both = jnp.dot(gather_ref[...], jnp.concatenate(rhs, axis=1), preferred_element_type=F32)
        done += [both[:, :128], both[:, 128:]]
    tail = pltpu.roll(done[0], 64, 1)
    for row in range(1, ROWS):
        here = done[row] if row == 2 else pltpu.roll(done[row], (32 * row - 64) % 128, 1)
        tail = jnp.where(lane < 32 * row, tail, here)
    for half in range(2):
        head = jnp.where(lane < 64, done[half], pltpu.roll(done[half + 2], 64, 1))
        o_ref[:, COLS * half : COLS * half + COLS, :] = head.reshape(SLOTS, COLS, 128).astype(BF16)
    o_ref[:, 2 * COLS :, :] = tail.reshape(SLOTS, COLS, 128).astype(BF16)


def main(low, own, high, prepared):
    return pl.pallas_call(
        main_kernel,
        out_shape=jax.ShapeDtypeStruct((SLOTS, BACK, 128), BF16),
        in_specs=[pl.BlockSpec(memory_space=VMEM)] * 12,
        out_specs=pl.BlockSpec(memory_space=VMEM),
        scratch_shapes=[
            VMEM((12, 256, HID), BF16),
            VMEM((10, 224, HID), BF16),
            VMEM((8, 192, HID), BF16),
            VMEM((6, 160, HID), BF16),
            VMEM((8, 192, 128), F32),
            VMEM((ROWS, 128, 128), F32),
        ],
        name="patch",
        compiler_params=pltpu.CompilerParams(vmem_limit_bytes=32 << 20),
    )(low, own, high, *prepared)


def unpack_kernel(p_ref, o_ref):
    pieces = p_ref[...].astype(F32)

    def turned(group):
        return pieces[:, COLS * group : COLS * group + COLS, :].reshape(128, 128).T

    heads, tail = [turned(0), turned(1)], turned(2)
    for row in range(ROWS):
        start = 64 if row >= 2 else 0
        o_ref[pl.ds(row, 64, stride=ROWS), :] = heads[row & 1][start : start + 64]
        o_ref[pl.ds(64 * ROWS + row, C - 64, stride=ROWS), :] = tail[32 * row : 32 * row + C - 64]


def unpack(pieces):
    return pl.pallas_call(
        unpack_kernel,
        out_shape=jax.ShapeDtypeStruct((C * ROWS, 128), F32),
        in_specs=[pl.BlockSpec(memory_space=VMEM)],
        out_specs=pl.BlockSpec(memory_space=VMEM),
        name="unpack",
        compiler_params=pltpu.CompilerParams(vmem_limit_bytes=8 << 20),
    )(pieces)


def on_device(trajectory, step_levels, in_weight, in_bias, conv_weight, cond_weight, out_weight):
    count = lax.axis_size("lat")
    forward = [(i, i + 1) for i in range(count - 1)]
    backward = [(b, a) for a, b in forward]
    pieces = pack(step_levels, trajectory.reshape(C * ROWS, 128))
    own = lax.all_to_all(pieces, "tm", 0, 0)
    prepared = tables(step_levels, in_weight.T, in_bias[None, :], cond_weight, out_weight, conv_weight)
    own, prepared = lax.optimization_barrier((own, prepared))
    low = lax.ppermute(own, "lat", forward)
    high = lax.ppermute(own, "lat", backward)
    done = main(low, own, high, prepared)
    back = lax.all_to_all(done, "tm", 0, 0)
    return unpack(back).reshape(1, C, ROWS, 128)


def solution(mesh):
    in_specs = (P("tm", None, "lat", None), P(), P(), P(), P(), P(), P())
    out_specs = P("tm", None, "lat", None)
    return jax.shard_map(on_device, mesh=mesh, in_specs=in_specs, out_specs=out_specs, check_vma=False)
```

```python
import functools

import jax
import jax.numpy as jnp
from jax import lax
from jax.experimental import pallas as pl
from jax.experimental.pallas import tpu as pltpu
from jax.sharding import PartitionSpec as P

LEVELS = 64
C = 84
HID = 256
SLOTS = 16
ROWS = 4
COLS = 8
PIECE = 48
BACK = 24

SIGMA_TOP = 1.0
SIGMA_LOW = 0.02
RHO = 7.0
ROOT_TOP = SIGMA_TOP ** (1.0 / RHO)
ROOT_LOW = SIGMA_LOW ** (1.0 / RHO)

F32 = jnp.float32
BF16 = jnp.bfloat16
VMEM = pltpu.VMEM
NT = (((1,), (1,)), ((), ()))
TN = (((0,), (0,)), ((), ()))


def iota(shape, dim):
    return lax.broadcasted_iota(jnp.int32, shape, dim)


def one_hot(mask):
    return jnp.where(mask, 1.0, 0.0).astype(BF16)


def sigma_of(level):
    root = ROOT_TOP + level.astype(F32) / (LEVELS - 1) * (ROOT_LOW - ROOT_TOP)
    square = root * root
    return square * square * square * root


def lane_of(channel, row):
    head = channel + jnp.where(row >= 2, 64, 0)
    tail = 128 + 32 * row + (channel - 64)
    return jnp.where(channel < 64, head, tail)


def pack_kernel(levels_hbm, x_hbm, o_ref, levels_ref, x_ref, sems):
    get_levels = pltpu.make_async_copy(levels_hbm, levels_ref, sems.at[0])
    get_x = pltpu.make_async_copy(x_hbm, x_ref, sems.at[1])
    get_levels.start()
    get_x.start()
    slot = lax.axis_index("tm")
    shape = (C * ROWS, 3 * 128)
    index, lane = iota(shape, 0), iota(shape, 1)
    channel, row = index >> 2, index & 3
    target = lane_of(channel, row)
    target = jnp.where(target < 128, target + 128 * (row & 1), target + 128)
    places = one_hot(lane == target)
    get_levels.wait()
    sigma = sigma_of(jnp.full((1, 128), levels_ref[slot], jnp.int32))
    scale = jnp.sqrt(sigma * sigma + 0.25)
    get_x.wait()
    scaled = pltpu.roll(x_ref[...] / scale, 4, 1).astype(BF16)
    packed = lax.dot_general(scaled, places, TN, preferred_element_type=F32)
    for window in range(SLOTS):
        start = COLS * window
        if window < SLOTS - 1:
            part = packed[start : start + 2 * COLS]
        else:
            part = jnp.concatenate([packed[start:], packed[:COLS]], axis=0)
        part = part.astype(BF16)
        for group in range(3):
            o_ref[window, 16 * group : 16 * group + 16, :] = part[:, 128 * group : 128 * group + 128]


def pack(levels, x):
    return pl.pallas_call(
        pack_kernel,
        out_shape=jax.ShapeDtypeStruct((SLOTS, PIECE, 128), BF16),
        in_specs=[pl.BlockSpec(memory_space=pltpu.HBM)] * 2,
        out_specs=pl.BlockSpec(memory_space=VMEM),
        scratch_shapes=[
            pltpu.SMEM((SLOTS + 1,), jnp.int32),
            VMEM((C * ROWS, 128), F32),
            pltpu.SemaphoreType.DMA((2,)),
        ],
        name="pack",
        compiler_params=pltpu.CompilerParams(vmem_limit_bytes=12000 << 10),
    )(*[pltpu.with_memory_space_constraint(v, pltpu.HBM) for v in (levels, x)])


def tables_kernel(levels_hbm, in_w_hbm, bias_hbm, cond_hbm, out_w_hbm, conv_hbm, film_ref, in_pack_ref, in_t_ref, out_t_ref, bias_ref, conv_ref, picks_ref, levels_ref, in_w_ref, cond_ref, out_w_ref, sems):
    sources = (levels_hbm, in_w_hbm, cond_hbm, out_w_hbm, bias_hbm, conv_hbm)
    targets = (levels_ref, in_w_ref, cond_ref, out_w_ref, bias_ref, conv_ref)
    copies = [pltpu.make_async_copy(a, b, sems.at[i]) for i, (a, b) in enumerate(zip(sources, targets))]
    for copy in copies:
        copy.start()
    to, frm = iota((256, 256), 0), iota((256, 256), 1)
    picks_ref[:256] = one_hot(((to >> 4) == (frm & 15)) & ((to & 15) == (frm >> 4)))
    to, frm = iota((128, 256), 0), iota((128, 256), 1) & 127
    picks_ref[256:384] = one_hot(((to >> 4) == (frm >> 4)) & ((frm & 15) < (to & 15)))
    picks_ref[384:] = one_hot(((to & 7) == (frm >> 4)) & ((frm & 15) <= (to >> 3)))
    copies[0].wait()
    place = iota((SLOTS, 128), 0)
    now = jnp.zeros((SLOTS, 128), jnp.int32)
    following = now
    for k in range(SLOTS):
        now = jnp.where(place == k, levels_ref[k], now)
        following = jnp.where(place == k, levels_ref[k + 1], following)
    now, following = sigma_of(now), sigma_of(following)
    variance = now * now + 0.25
    root = jnp.sqrt(variance)
    ratio = (following - now) / now
    film_ref[4, :, :128] = 1.0 / root
    film_ref[4, :, 128:] = root
    film_ref[5, :, :128] = (1.0 - 0.25 / variance) * ratio
    film_ref[5, :, 128:] = 0.5 * now / root * ratio
    j = iota((SLOTS, 128), 1).astype(F32)
    frequency = jnp.exp(j * (jnp.log(F32(100.0)) / 128.0))
    phases = jnp.log(now) / 4.0 * frequency
    embedding = jnp.concatenate([jnp.cos(phases), jnp.sin(phases)], axis=1).astype(BF16)
    copies[1].wait()
    copies[2].wait()
    copies[3].wait()
    conditions = jnp.dot(embedding, cond_ref[...], preferred_element_type=F32)
    film_ref[0] = 0.5 * (1.0 + conditions[:, 0:256])
    film_ref[1] = 0.5 * conditions[:, 256:512]
    film_ref[2] = 0.5 * (1.0 + conditions[:, 512:768])
    film_ref[3] = 0.5 * conditions[:, 768:1024]
    channel, lane = iota((C, 256), 0), iota((C, 256), 1)
    for row in range(ROWS):
        pick = one_hot(lane == lane_of(channel, row))
        in_pack_ref[row] = lax.dot_general(pick, in_w_ref[...], TN, preferred_element_type=F32).astype(BF16)
    eye = one_hot(iota((C, 128), 0) == iota((C, 128), 1))
    in_t_ref[...] = lax.dot_general(eye, in_w_ref[...], TN, preferred_element_type=F32).astype(BF16)
    out_t_ref[...] = lax.dot_general(out_w_ref[...], eye, TN, preferred_element_type=F32).astype(BF16)
    copies[4].wait()
    copies[5].wait()


def tables(levels, in_weight_t, in_bias, cond_weight, out_weight, conv_weight):
    return pl.pallas_call(
        tables_kernel,
        out_shape=[
            jax.ShapeDtypeStruct((6, SLOTS, HID), F32),
            jax.ShapeDtypeStruct((ROWS, 256, HID), BF16),
            jax.ShapeDtypeStruct((128, HID), BF16),
            jax.ShapeDtypeStruct((HID, 128), BF16),
            jax.ShapeDtypeStruct((1, HID), F32),
            jax.ShapeDtypeStruct((2, HID, 9 * HID), BF16),
            jax.ShapeDtypeStruct((512, 256), BF16),
        ],
        in_specs=[pl.BlockSpec(memory_space=pltpu.HBM)] * 6,
        out_specs=[pl.BlockSpec(memory_space=VMEM)] * 7,
        scratch_shapes=[
            pltpu.SMEM((SLOTS + 1,), jnp.int32),
            VMEM((C, HID), BF16),
            VMEM((256, 1024), BF16),
            VMEM((C, HID), BF16),
            pltpu.SemaphoreType.DMA((6,)),
        ],
        name="tables",
        compiler_params=pltpu.CompilerParams(vmem_limit_bytes=12000 << 10),
    )(*[pltpu.with_memory_space_constraint(v, pltpu.HBM) for v in (levels, in_weight_t, in_bias, cond_weight, out_weight, conv_weight)])


def split(value):
    high = value.astype(BF16)
    return high, (value - high.astype(F32)).astype(BF16)


def convolve(ref, top, rows, cells, weight):
    parts = []
    for a in range(3):
        for b in range(3):
            view = ref[top + a : top + a + rows, 16 * b : 16 * b + cells, :]
            parts.append(view.reshape(rows * cells, HID))
    return lax.dot_general(jnp.concatenate(parts, axis=1), weight, NT, preferred_element_type=F32)


def film(response, scale, shift):
    cells = response.shape[0] // SLOTS
    half = response.reshape(cells, SLOTS, HID) * scale[None] + shift[None]
    return (half * jnp.tanh(half) + half).reshape(cells * SLOTS, HID)


def halves(value):
    high, low = split(value)
    return jnp.concatenate([high, low], axis=0)


def main_kernel(near_ref, own_ref, far_ref, film_ref, in_pack_ref, in_t_ref, out_t_ref, bias_ref, conv_ref, picks_ref, o_ref, h0, h1, g0, g1, x1, s2):
    place = lax.axis_index("lat")
    count = lax.axis_size("lat")
    inside_low = jnp.where(place > 0, 1.0, 0.0).astype(F32)
    inside_high = jnp.where(place < count - 1, 1.0, 0.0).astype(F32)
    gates = (inside_low, F32(1.0), inside_high)
    bias = bias_ref[...]
    lane = iota((1, 128), 1)
    first = iota((1, SLOTS, 128), 1) == 0

    def gate_of(row):
        return inside_low if row < 0 else inside_high if row >= ROWS else F32(1.0)

    odd = (place & 1) == 1
    near, far = near_ref[...], far_ref[...]
    blocks = [
        [value[:, 16 * group : 16 * group + 16, :].reshape(256, 128) for group in range(3)]
        for value in (jnp.where(odd, near, far), own_ref[...], jnp.where(odd, far, near))
    ]
    swap = picks_ref[:256]

    def swapped(left, right):
        both = jnp.dot(swap, jnp.concatenate([left, right], axis=1), preferred_element_type=F32)
        return both[:, :128], both[:, 128:]

    heads = [swapped(block[0], block[1]) for block in blocks]
    tails = [*swapped(blocks[0][2], blocks[1][2])]
    tails.append(jnp.dot(swap, blocks[2][2], preferred_element_type=F32))

    for row in range(ROWS):
        lhs = jnp.concatenate(
            [jnp.concatenate([heads[at][row & 1], tails[at]], axis=1).astype(BF16) for at in range(3)], axis=0
        )
        hidden = jnp.dot(lhs, in_pack_ref[row], preferred_element_type=F32)
        for at in range(3):
            i = 4 * at + row
            h0[i] = (hidden[256 * at : 256 * at + 256] + bias * gates[at]).astype(BF16)
            if 2 <= i < 10:
                head, tail = heads[at][row & 1][32:224], tails[at][32:224]
                if row >= 2:
                    head = pltpu.roll(head, 64, 1)
                if row != 2:
                    tail = pltpu.roll(tail, (64 - 32 * row) % 128, 1)
                value = jnp.where(lane < 64, head, jnp.where(lane < C, tail, 0.0))
                x1[i - 2] = (value.reshape(12, SLOTS, 128) * film_ref[4, :, 128:][None]).reshape(192, 128)

    for top in (0, 5):
        response = convolve(h0, top, 5, 224, conv_ref[0])
        for at in range(5):
            gate = gate_of(top + at - 3)
            hidden = film(response[224 * at : 224 * at + 224], film_ref[0] * gate, film_ref[1] * gate)
            h1[top + at] = hidden.astype(BF16)

    for top in (0, 4):
        response = convolve(h1, top, 4, 192, conv_ref[1])
        hidden = h1[top + 1 : top + 5, 16:208, :].reshape(768, HID).astype(F32)
        hidden = hidden + film(response, film_ref[2], film_ref[3])
        network = jnp.dot(hidden.astype(BF16), out_t_ref[...], preferred_element_type=F32)
        x = x1[top : top + 4].reshape(48, SLOTS, 128)
        anchor = jnp.where(first, x, 0.0)
        drift = film_ref[5, :, :128][None] * x - film_ref[5, :, 128:][None] * network.reshape(48, SLOTS, 128) + anchor
        drift = drift.reshape(768, 128)
        earlier = []
        for pair in range(3):
            rhs = [halves(drift[256 * pair + 128 * k : 256 * pair + 128 * k + 128]) for k in range(2)]
            both = jnp.dot(picks_ref[256:384], jnp.concatenate(rhs, axis=1), preferred_element_type=F32)
            earlier += [both[:, :128], both[:, 128:]]
        state = jnp.concatenate(earlier, axis=0).reshape(48, SLOTS, 128) + anchor
        scaled = []
        for at in range(4):
            i = top + at
            here = state[12 * at : 12 * at + 12]
            if 2 <= i < 6:
                s2[i - 2] = here[2:10].reshape(128, 128)
            scaled.append((here * (film_ref[4, :, :128] * gate_of(i - 2))[None]).reshape(192, 128).astype(BF16))
        hidden = jnp.dot(jnp.concatenate(scaled, axis=0), in_t_ref[...], preferred_element_type=F32)
        for at in range(4):
            g0[top + at] = (hidden[192 * at : 192 * at + 192] + bias * gate_of(top + at - 2)).astype(BF16)

    for top in (0, 3):
        response = convolve(g0, top, 3, 160, conv_ref[0])
        for at in range(3):
            gate = gate_of(top + at - 1)
            hidden = film(response[160 * at : 160 * at + 160], film_ref[0] * gate, film_ref[1] * gate)
            g1[top + at] = hidden.astype(BF16)

    response = convolve(g1, 0, 4, 128, conv_ref[1])
    hidden = g1[1:5, 16:144, :].reshape(512, HID).astype(F32)
    hidden = hidden + film(response, film_ref[2], film_ref[3])
    network = jnp.dot(hidden.astype(BF16), out_t_ref[...], preferred_element_type=F32)
    state = s2[...].reshape(32, SLOTS, 128)
    anchor = jnp.where(first, state, 0.0)
    drift = film_ref[5, :, :128][None] * state - film_ref[5, :, 128:][None] * network.reshape(32, SLOTS, 128) + anchor
    drift = drift.reshape(512, 128)
    done = []
    for pair in range(2):
        rhs = [halves(drift[256 * pair + 128 * k : 256 * pair + 128 * k + 128]) for k in range(2)]
        both = jnp.dot(picks_ref[384:], jnp.concatenate(rhs, axis=1), preferred_element_type=F32)
        done += [both[:, :128], both[:, 128:]]
    tail = pltpu.roll(done[0], 64, 1)
    for row in range(1, ROWS):
        here = done[row] if row == 2 else pltpu.roll(done[row], (32 * row - 64) % 128, 1)
        tail = jnp.where(lane < 32 * row, tail, here)
    for half in range(2):
        head = jnp.where(lane < 64, done[half], pltpu.roll(done[half + 2], 64, 1))
        o_ref[:, COLS * half : COLS * half + COLS, :] = head.reshape(SLOTS, COLS, 128).astype(BF16)
    o_ref[:, 2 * COLS :, :] = tail.reshape(SLOTS, COLS, 128).astype(BF16)


def main(near, own, far, prepared):
    return pl.pallas_call(
        main_kernel,
        out_shape=jax.ShapeDtypeStruct((SLOTS, BACK, 128), BF16),
        in_specs=[pl.BlockSpec(memory_space=VMEM)] * 10,
        out_specs=pl.BlockSpec(memory_space=VMEM),
        scratch_shapes=[
            VMEM((12, 256, HID), BF16),
            VMEM((10, 224, HID), BF16),
            VMEM((8, 192, HID), BF16),
            VMEM((6, 160, HID), BF16),
            VMEM((8, 192, 128), F32),
            VMEM((ROWS, 128, 128), F32),
        ],
        name="patch",
        compiler_params=pltpu.CompilerParams(vmem_limit_bytes=32 << 20),
    )(near, own, far, *prepared)


def unpack_kernel(p_ref, o_ref):
    pieces = p_ref[...].astype(F32)

    def turned(group):
        return pieces[:, COLS * group : COLS * group + COLS, :].reshape(128, 128).T

    heads, tail = [turned(0), turned(1)], turned(2)
    for row in range(ROWS):
        start = 64 if row >= 2 else 0
        o_ref[pl.ds(row, 64, stride=ROWS), :] = heads[row & 1][start : start + 64]
        o_ref[pl.ds(64 * ROWS + row, C - 64, stride=ROWS), :] = tail[32 * row : 32 * row + C - 64]


def unpack(pieces):
    return pl.pallas_call(
        unpack_kernel,
        out_shape=jax.ShapeDtypeStruct((C * ROWS, 128), F32),
        in_specs=[pl.BlockSpec(memory_space=VMEM)],
        out_specs=pl.BlockSpec(memory_space=VMEM),
        name="unpack",
        compiler_params=pltpu.CompilerParams(vmem_limit_bytes=8 << 20),
    )(pieces)


def on_device(trajectory, step_levels, in_weight, in_bias, conv_weight, cond_weight, out_weight):
    count = lax.axis_size("lat")
    near_pairs = [(i, i ^ 1) for i in range(count)]
    far_pairs = [pair for i in range(1, count - 1, 2) for pair in ((i, i + 1), (i + 1, i))]
    pieces = pack(step_levels, trajectory.reshape(C * ROWS, 128))
    own = lax.all_to_all(pieces, "tm", 0, 0)
    prepared = tables(step_levels, in_weight.T, in_bias[None, :], cond_weight, out_weight, conv_weight)
    own, prepared = lax.optimization_barrier((own, prepared))
    near = lax.ppermute(own, "lat", near_pairs)
    far = lax.ppermute(own, "lat", far_pairs)
    done = main(near, own, far, prepared)
    back = lax.all_to_all(done, "tm", 0, 0)
    return unpack(back).reshape(1, C, ROWS, 128)


def solution(mesh):
    in_specs = (P("tm", None, "lat", None), P(), P(), P(), P(), P(), P())
    out_specs = P("tm", None, "lat", None)
    return jax.shard_map(on_device, mesh=mesh, in_specs=in_specs, out_specs=out_specs, check_vma=False)
```

```python
import functools

import jax
import jax.numpy as jnp
from jax import lax
from jax.experimental import pallas as pl
from jax.experimental.pallas import tpu as pltpu
from jax.sharding import PartitionSpec as P

LEVELS = 64
C = 84
HID = 256
SLOTS = 16
ROWS = 4
COLS = 8
PIECE = 48
BACK = 24
SWAP, BEFORE, UPTO, IN_T, OUT_T = slice(0, 256), slice(256, 384), slice(384, 512), slice(512, 640), slice(640, 768)
IN_PACK = 768

SIGMA_TOP = 1.0
SIGMA_LOW = 0.02
RHO = 7.0
ROOT_TOP = SIGMA_TOP ** (1.0 / RHO)
ROOT_LOW = SIGMA_LOW ** (1.0 / RHO)

F32 = jnp.float32
BF16 = jnp.bfloat16
VMEM = pltpu.VMEM
NT = (((1,), (1,)), ((), ()))
TN = (((0,), (0,)), ((), ()))


def iota(shape, dim):
    return lax.broadcasted_iota(jnp.int32, shape, dim)


def one_hot(mask):
    return jnp.where(mask, 1.0, 0.0).astype(BF16)


def sigma_of(level):
    root = ROOT_TOP + level.astype(F32) / (LEVELS - 1) * (ROOT_LOW - ROOT_TOP)
    square = root * root
    return square * square * square * root


def lane_of(channel, row):
    head = channel + jnp.where(row >= 2, 64, 0)
    tail = 128 + 32 * row + (channel - 64)
    return jnp.where(channel < 64, head, tail)


def pack_kernel(levels_hbm, x_hbm, o_ref, levels_ref, x_ref, sems):
    get_levels = pltpu.make_async_copy(levels_hbm, levels_ref, sems.at[0])
    get_x = pltpu.make_async_copy(x_hbm, x_ref, sems.at[1])
    get_levels.start()
    get_x.start()
    slot = lax.axis_index("tm")
    shape = (C * ROWS, 3 * 128)
    index, lane = iota(shape, 0), iota(shape, 1)
    channel, row = index >> 2, index & 3
    target = lane_of(channel, row)
    target = jnp.where(target < 128, target + 128 * (row & 1), target + 128)
    places = one_hot(lane == target)
    get_levels.wait()
    sigma = sigma_of(jnp.full((1, 128), levels_ref[slot], jnp.int32))
    scale = jnp.sqrt(sigma * sigma + 0.25)
    get_x.wait()
    scaled = pltpu.roll(x_ref[...] / scale, 4, 1).astype(BF16)
    packed = lax.dot_general(scaled, places, TN, preferred_element_type=F32)
    for window in range(SLOTS):
        start = COLS * window
        if window < SLOTS - 1:
            part = packed[start : start + 2 * COLS]
        else:
            part = jnp.concatenate([packed[start:], packed[:COLS]], axis=0)
        part = part.astype(BF16)
        for group in range(3):
            o_ref[window, 16 * group : 16 * group + 16, :] = part[:, 128 * group : 128 * group + 128]


def pack(levels, x):
    return pl.pallas_call(
        pack_kernel,
        out_shape=jax.ShapeDtypeStruct((SLOTS, PIECE, 128), BF16),
        in_specs=[pl.BlockSpec(memory_space=pltpu.HBM)] * 2,
        out_specs=pl.BlockSpec(memory_space=VMEM),
        scratch_shapes=[
            pltpu.SMEM((SLOTS + 1,), jnp.int32),
            VMEM((C * ROWS, 128), F32),
            pltpu.SemaphoreType.DMA((2,)),
        ],
        name="pack",
        compiler_params=pltpu.CompilerParams(vmem_limit_bytes=12000 << 10),
    )(*[pltpu.with_memory_space_constraint(v, pltpu.HBM) for v in (levels, x)])


def tables_kernel(levels_hbm, in_w_hbm, bias_hbm, cond_hbm, out_w_hbm, conv_hbm, film_ref, picks_ref, filter_ref, levels_ref, in_w_ref, bias_ref, cond_ref, out_w_ref, conv_ref, sems):
    sources = (levels_hbm, in_w_hbm, cond_hbm, out_w_hbm, bias_hbm, conv_hbm)
    targets = (levels_ref, in_w_ref, cond_ref, out_w_ref, bias_ref, conv_ref)
    copies = [pltpu.make_async_copy(a, b, sems.at[i]) for i, (a, b) in enumerate(zip(sources, targets))]
    for copy in copies:
        copy.start()
    to, frm = iota((256, 256), 0), iota((256, 256), 1)
    picks_ref[SWAP] = one_hot(((to >> 4) == (frm & 15)) & ((to & 15) == (frm >> 4)))
    to, frm = iota((128, 256), 0), iota((128, 256), 1) & 127
    picks_ref[BEFORE] = one_hot(((to >> 4) == (frm >> 4)) & ((frm & 15) < (to & 15)))
    cell = frm >> 4
    column = ((cell & 3) << 1) + (cell >> 2)
    picks_ref[UPTO] = one_hot(((to & 7) == column) & ((frm & 15) <= (to >> 3)))
    copies[0].wait()
    place = iota((SLOTS, 128), 0)
    now = jnp.zeros((SLOTS, 128), jnp.int32)
    following = now
    for k in range(SLOTS):
        now = jnp.where(place == k, levels_ref[k], now)
        following = jnp.where(place == k, levels_ref[k + 1], following)
    now, following = sigma_of(now), sigma_of(following)
    variance = now * now + 0.25
    root = jnp.sqrt(variance)
    ratio = (following - now) / now
    film_ref[4, :, :128] = 1.0 / root
    film_ref[4, :, 128:] = root
    film_ref[5, :, :128] = (1.0 - 0.25 / variance) * ratio
    film_ref[5, :, 128:] = 0.5 * now / root * ratio
    j = iota((SLOTS, 128), 1).astype(F32)
    frequency = jnp.exp(j * (jnp.log(F32(100.0)) / 128.0))
    phases = jnp.log(now) / 4.0 * frequency
    embedding = jnp.concatenate([jnp.cos(phases), jnp.sin(phases)], axis=1).astype(BF16)
    for copy in copies[1:5]:
        copy.wait()
    film_ref[6] = jnp.broadcast_to(bias_ref[...], (SLOTS, HID))
    conditions = jnp.dot(embedding, cond_ref[...], preferred_element_type=F32)
    film_ref[0] = 0.5 * (1.0 + conditions[:, 0:256])
    film_ref[1] = 0.5 * conditions[:, 256:512]
    film_ref[2] = 0.5 * (1.0 + conditions[:, 512:768])
    film_ref[3] = 0.5 * conditions[:, 768:1024]
    channel, lane = iota((C, 256), 0), iota((C, 256), 1)
    for row in range(ROWS):
        pick = one_hot(lane == lane_of(channel, row))
        packed = lax.dot_general(pick, in_w_ref[...], TN, preferred_element_type=F32)
        picks_ref[IN_PACK + 256 * row : IN_PACK + 256 * row + 256] = packed.astype(BF16)
    eye = one_hot(iota((C, 128), 0) == iota((C, 128), 1))
    picks_ref[IN_T] = lax.dot_general(eye, in_w_ref[...], TN, preferred_element_type=F32).astype(BF16)
    picks_ref[OUT_T] = lax.dot_general(eye, out_w_ref[...], TN, preferred_element_type=F32).astype(BF16)
    copies[5].wait()
    for layer in range(2):
        for a in range(3):
            west, mid, east = [conv_ref[layer, :, HID * (3 * a + b) : HID * (3 * a + b) + HID] for b in range(3)]
            lanes = slice(HID * a, HID * a + HID)
            outer = 0.5 * (west.astype(F32) + east.astype(F32))
            inner = 0.5 * mid.astype(F32)
            filter_ref[layer, 0, :, lanes] = west
            filter_ref[layer, 1, :, lanes] = (outer + inner).astype(BF16)
            filter_ref[layer, 2, :, lanes] = (outer - inner).astype(BF16)
            filter_ref[layer, 3, :, lanes] = east


def tables(levels, in_weight_t, in_bias, cond_weight, out_weight, conv_weight):
    return pl.pallas_call(
        tables_kernel,
        out_shape=[
            jax.ShapeDtypeStruct((7, SLOTS, HID), F32),
            jax.ShapeDtypeStruct((IN_PACK + 1024, 256), BF16),
            jax.ShapeDtypeStruct((2, 4, HID, 3 * HID), BF16),
        ],
        in_specs=[pl.BlockSpec(memory_space=pltpu.HBM)] * 6,
        out_specs=[pl.BlockSpec(memory_space=VMEM)] * 3,
        scratch_shapes=[
            pltpu.SMEM((SLOTS + 1,), jnp.int32),
            VMEM((C, HID), BF16),
            VMEM((1, HID), F32),
            VMEM((256, 1024), BF16),
            VMEM((C, HID), BF16),
            VMEM((2, HID, 9 * HID), BF16),
            pltpu.SemaphoreType.DMA((6,)),
        ],
        name="tables",
        compiler_params=pltpu.CompilerParams(vmem_limit_bytes=24 << 20),
    )(*[pltpu.with_memory_space_constraint(v, pltpu.HBM) for v in (levels, in_weight_t, in_bias, cond_weight, out_weight, conv_weight)])


def split(value):
    high = value.astype(BF16)
    return high, (value - high.astype(F32)).astype(BF16)


def convolve(ref, top, rows, pairs, filters):
    parts = []
    for kind in range(4):
        views = [ref[kind, top + a : top + a + rows].reshape(rows * pairs * SLOTS, HID) for a in range(3)]
        lhs = jnp.concatenate(views, axis=1)
        parts.append(lax.dot_general(lhs, filters[kind], NT, preferred_element_type=F32))
    shape = (rows, pairs, SLOTS, HID)
    even = parts[0] + (parts[1] + parts[2])
    odd = (parts[1] - parts[2]) - parts[3]
    return even.reshape(shape), odd.reshape(shape)


def transform(ref, row, even, odd):
    size = (even.shape[0] - 1) * SLOTS
    values = (even[:-1] - even[1:], odd[:-1] + even[1:], even[1:] - odd[:-1], odd[:-1] - odd[1:])
    for kind, value in enumerate(values):
        ref[kind, row] = value.reshape(size, HID).astype(BF16)


def film(response, scale, shift):
    half = response * scale + shift
    return half * jnp.tanh(half) + half


def halves(value):
    high, low = split(value)
    return jnp.concatenate([high, low], axis=0)


def columns(value, count):
    pairs = value.reshape(count // 2, 2, SLOTS, value.shape[1])
    return pairs[:, 0], pairs[:, 1]


def scan(picks, drift):
    sums = []
    for start in range(0, drift.shape[0], 256):
        rhs = [halves(drift[start + at : start + at + 128]) for at in (0, 128)]
        both = jnp.dot(picks, jnp.concatenate(rhs, axis=1), preferred_element_type=F32)
        sums += [both[:, :128], both[:, 128:]]
    return sums


def main_kernel(near_ref, own_ref, far_ref, film_ref, picks_ref, filter_ref, o_ref, h0, h1, g0, g1, h1_even, h1_odd, g1_even, g1_odd, x_even, x_odd, s_even, s_odd):
    place = lax.axis_index("lat")
    count = lax.axis_size("lat")
    inside_low = jnp.where(place > 0, 1.0, 0.0).astype(F32)
    inside_high = jnp.where(place < count - 1, 1.0, 0.0).astype(F32)
    gates = (inside_low, F32(1.0), inside_high)
    bias = film_ref[6]
    inverse, root = film_ref[4, :, :128], film_ref[4, :, 128:]
    keep, gain = film_ref[5, :, :128], film_ref[5, :, 128:]
    lane = iota((1, 128), 1)
    first = iota((1, 1, SLOTS, 128), 2) == 0

    def gate_of(row):
        return inside_low if row < 0 else inside_high if row >= ROWS else F32(1.0)

    swap_odd = (place & 1) == 1
    near, far = near_ref[...], far_ref[...]
    blocks = [
        [value[:, 16 * group : 16 * group + 16, :].reshape(256, 128) for group in range(3)]
        for value in (jnp.where(swap_odd, near, far), own_ref[...], jnp.where(swap_odd, far, near))
    ]
    swap = picks_ref[SWAP]

    def swapped(left, right):
        both = jnp.dot(swap, jnp.concatenate([left, right], axis=1), preferred_element_type=F32)
        return both[:, :128], both[:, 128:]

    heads = [swapped(block[0], block[1]) for block in blocks]
    tails = [*swapped(blocks[0][2], blocks[1][2])]
    tails.append(jnp.dot(swap, blocks[2][2], preferred_element_type=F32))

    for row in range(ROWS):
        lhs = jnp.concatenate(
            [jnp.concatenate([heads[at][row & 1], tails[at]], axis=1).astype(BF16) for at in range(3)], axis=0
        )
        weight = picks_ref[IN_PACK + 256 * row : IN_PACK + 256 * row + 256]
        hidden = jnp.dot(lhs, weight, preferred_element_type=F32)
        for at in range(3):
            i = 4 * at + row
            even, odd = columns(hidden[256 * at : 256 * at + 256], 16)
            shift = (bias * gates[at])[None]
            transform(h0, i, even + shift, odd + shift)
            if 2 <= i < 10:
                head, tail = heads[at][row & 1][32:224], tails[at][32:224]
                if row >= 2:
                    head = pltpu.roll(head, 64, 1)
                if row != 2:
                    tail = pltpu.roll(tail, (64 - 32 * row) % 128, 1)
                value = jnp.where(lane < 64, head, jnp.where(lane < C, tail, 0.0))
                even, odd = columns(value, 12)
                x_even[i - 2], x_odd[i - 2] = even * root[None], odd * root[None]

    for top in range(0, 10, 5):
        even, odd = convolve(h0, top, 5, 7, filter_ref.at[0])
        for at in range(5):
            i = top + at
            scale, shift = film_ref[0] * gate_of(i - 3), film_ref[1] * gate_of(i - 3)
            here_even, here_odd = film(even[at], scale[None], shift[None]), film(odd[at], scale[None], shift[None])
            transform(h1, i, here_even, here_odd)
            if 1 <= i < 9:
                h1_even[i - 1] = here_odd[:-1].astype(BF16)
                h1_odd[i - 1] = here_even[1:].astype(BF16)

    def network(even, odd):
        hidden = jnp.concatenate([even.reshape(-1, HID), odd.reshape(-1, HID)], axis=0).astype(BF16)
        return lax.dot_general(hidden, picks_ref[OUT_T], NT, preferred_element_type=F32)

    film_two = film_ref[2][None, None], film_ref[3][None, None]

    for top in range(0, 8, 4):
        even, odd = convolve(h1, top, 4, 6, filter_ref.at[1])
        even = h1_even[top : top + 4].astype(F32) + film(even, *film_two)
        odd = h1_odd[top : top + 4].astype(F32) + film(odd, *film_two)
        x = jnp.concatenate([x_even[top : top + 4], x_odd[top : top + 4]], axis=0)
        anchor = jnp.where(first, x, 0.0)
        drift = keep * x - gain * network(even, odd).reshape(8, 6, SLOTS, 128) + anchor
        state = jnp.concatenate(scan(picks_ref[BEFORE], drift.reshape(768, 128)), axis=0)
        state = state.reshape(8, 6, SLOTS, 128) + anchor
        scaled = []
        for parity in range(2):
            for at in range(4):
                i = top + at
                here = state[4 * parity + at]
                if 2 <= i < 6:
                    if parity == 0:
                        s_even[i - 2] = here[1:5]
                    else:
                        s_odd[i - 2] = here[1:5]
                scaled.append((here * (inverse * gate_of(i - 2))[None]).reshape(96, 128).astype(BF16))
        hidden = jnp.dot(jnp.concatenate(scaled, axis=0), picks_ref[IN_T], preferred_element_type=F32)
        hidden = hidden.reshape(8, 6, SLOTS, HID)
        for at in range(4):
            shift = (bias * gate_of(top + at - 2))[None]
            transform(g0, top + at, hidden[at] + shift, hidden[4 + at] + shift)

    for top in range(0, 6, 3):
        even, odd = convolve(g0, top, 3, 5, filter_ref.at[0])
        for at in range(3):
            i = top + at
            scale, shift = film_ref[0] * gate_of(i - 1), film_ref[1] * gate_of(i - 1)
            here_even, here_odd = film(even[at], scale[None], shift[None]), film(odd[at], scale[None], shift[None])
            transform(g1, i, here_even, here_odd)
            if 1 <= i < 5:
                g1_even[i - 1] = here_odd[:-1].astype(BF16)
                g1_odd[i - 1] = here_even[1:].astype(BF16)

    even, odd = convolve(g1, 0, 4, 4, filter_ref.at[1])
    even = g1_even[...].astype(F32) + film(even, *film_two)
    odd = g1_odd[...].astype(F32) + film(odd, *film_two)
    state = jnp.concatenate([s_even[...], s_odd[...]], axis=0)
    drift = keep * state - gain * network(even, odd).reshape(8, 4, SLOTS, 128) + jnp.where(first, state, 0.0)
    drift = drift.reshape(2, 4, 64, 128)
    done = scan(picks_ref[UPTO], jnp.concatenate([drift[0], drift[1]], axis=1).reshape(512, 128))
    tail = pltpu.roll(done[0], 64, 1)
    for row in range(1, ROWS):
        here = done[row] if row == 2 else pltpu.roll(done[row], (32 * row - 64) % 128, 1)
        tail = jnp.where(lane < 32 * row, tail, here)
    for half in range(2):
        head = jnp.where(lane < 64, done[half], pltpu.roll(done[half + 2], 64, 1))
        o_ref[:, COLS * half : COLS * half + COLS, :] = head.reshape(SLOTS, COLS, 128).astype(BF16)
    o_ref[:, 2 * COLS :, :] = tail.reshape(SLOTS, COLS, 128).astype(BF16)


def main(near, own, far, prepared):
    return pl.pallas_call(
        main_kernel,
        out_shape=jax.ShapeDtypeStruct((SLOTS, BACK, 128), BF16),
        in_specs=[pl.BlockSpec(memory_space=VMEM)] * 6,
        out_specs=pl.BlockSpec(memory_space=VMEM),
        scratch_shapes=[
            VMEM((4, 12, 112, HID), BF16),
            VMEM((4, 10, 96, HID), BF16),
            VMEM((4, 8, 80, HID), BF16),
            VMEM((4, 6, 64, HID), BF16),
            *[VMEM((8, 6, SLOTS, HID), BF16)] * 2,
            *[VMEM((ROWS, 4, SLOTS, HID), BF16)] * 2,
            *[VMEM((8, 6, SLOTS, 128), F32)] * 2,
            *[VMEM((ROWS, 4, SLOTS, 128), F32)] * 2,
        ],
        name="patch",
        compiler_params=pltpu.CompilerParams(vmem_limit_bytes=32 << 20),
    )(near, own, far, *prepared)


def unpack_kernel(p_ref, o_ref):
    pieces = p_ref[...].astype(F32)

    def turned(group):
        return pieces[:, COLS * group : COLS * group + COLS, :].reshape(128, 128).T

    heads, tail = [turned(0), turned(1)], turned(2)
    for row in range(ROWS):
        start = 64 if row >= 2 else 0
        o_ref[pl.ds(row, 64, stride=ROWS), :] = heads[row & 1][start : start + 64]
        o_ref[pl.ds(64 * ROWS + row, C - 64, stride=ROWS), :] = tail[32 * row : 32 * row + C - 64]


def unpack(pieces):
    return pl.pallas_call(
        unpack_kernel,
        out_shape=jax.ShapeDtypeStruct((C * ROWS, 128), F32),
        in_specs=[pl.BlockSpec(memory_space=VMEM)],
        out_specs=pl.BlockSpec(memory_space=VMEM),
        name="unpack",
        compiler_params=pltpu.CompilerParams(vmem_limit_bytes=8 << 20),
    )(pieces)


def on_device(trajectory, step_levels, in_weight, in_bias, conv_weight, cond_weight, out_weight):
    count = lax.axis_size("lat")
    near_pairs = [(i, i ^ 1) for i in range(count)]
    far_pairs = [pair for i in range(1, count - 1, 2) for pair in ((i, i + 1), (i + 1, i))]
    pieces = pack(step_levels, trajectory.reshape(C * ROWS, 128))
    own = lax.all_to_all(pieces, "tm", 0, 0)
    prepared = tables(step_levels, in_weight.T, in_bias[None, :], cond_weight, out_weight, conv_weight)
    own, prepared = lax.optimization_barrier((own, prepared))
    near = lax.ppermute(own, "lat", near_pairs)
    far = lax.ppermute(own, "lat", far_pairs)
    done = main(near, own, far, prepared)
    back = lax.all_to_all(done, "tm", 0, 0)
    return unpack(back).reshape(1, C, ROWS, 128)


def solution(mesh):
    in_specs = (P("tm", None, "lat", None), P(), P(), P(), P(), P(), P())
    out_specs = P("tm", None, "lat", None)
    return jax.shard_map(on_device, mesh=mesh, in_specs=in_specs, out_specs=out_specs, check_vma=False)
```

```python
import functools

import jax
import jax.numpy as jnp
from jax import lax
from jax.experimental import pallas as pl
from jax.experimental.pallas import tpu as pltpu
from jax.sharding import PartitionSpec as P

LEVELS = 64
C = 84
HID = 256
SLOTS = 16
ROWS = 4
COLS = 8
PIECE = 48
BACK = 24
SWAP, BEFORE, UPTO, IN_T, OUT_T = slice(0, 256), slice(256, 384), slice(384, 512), slice(512, 640), slice(640, 768)
IN_PACK = 768
LIMIT = 32 << 20

SIGMA_TOP = 1.0
SIGMA_LOW = 0.02
RHO = 7.0
ROOT_TOP = SIGMA_TOP ** (1.0 / RHO)
ROOT_LOW = SIGMA_LOW ** (1.0 / RHO)

F32 = jnp.float32
BF16 = jnp.bfloat16
VMEM = pltpu.VMEM
NT = (((1,), (1,)), ((), ()))
TN = (((0,), (0,)), ((), ()))


def iota(shape, dim):
    return lax.broadcasted_iota(jnp.int32, shape, dim)


def one_hot(mask):
    return jnp.where(mask, 1.0, 0.0).astype(BF16)


def sigma_of(level):
    root = ROOT_TOP + level.astype(F32) / (LEVELS - 1) * (ROOT_LOW - ROOT_TOP)
    square = root * root
    return square * square * square * root


def lane_of(channel, row):
    head = channel + jnp.where(row >= 2, 64, 0)
    tail = 128 + 32 * row + (channel - 64)
    return jnp.where(channel < 64, head, tail)


def pack_kernel(levels_hbm, x_hbm, o_ref, levels_ref, x_ref, sems):
    get_levels = pltpu.make_async_copy(levels_hbm, levels_ref, sems.at[0])
    get_x = pltpu.make_async_copy(x_hbm, x_ref, sems.at[1])
    get_levels.start()
    get_x.start()
    slot = lax.axis_index("tm")
    shape = (C * ROWS, 3 * 128)
    index, lane = iota(shape, 0), iota(shape, 1)
    channel, row = index >> 2, index & 3
    target = lane_of(channel, row)
    target = jnp.where(target < 128, target + 128 * (row & 1), target + 128)
    places = one_hot(lane == target)
    get_levels.wait()
    sigma = sigma_of(jnp.full((1, 128), levels_ref[slot], jnp.int32))
    scale = jnp.sqrt(sigma * sigma + 0.25)
    get_x.wait()
    scaled = pltpu.roll(x_ref[...] / scale, 4, 1).astype(BF16)
    packed = lax.dot_general(scaled, places, TN, preferred_element_type=F32)
    for window in range(SLOTS):
        start = COLS * window
        if window < SLOTS - 1:
            part = packed[start : start + 2 * COLS]
        else:
            part = jnp.concatenate([packed[start:], packed[:COLS]], axis=0)
        part = part.astype(BF16)
        for group in range(3):
            o_ref[window, 16 * group : 16 * group + 16, :] = part[:, 128 * group : 128 * group + 128]


def pack(levels, x):
    return pl.pallas_call(
        pack_kernel,
        out_shape=jax.ShapeDtypeStruct((SLOTS, PIECE, 128), BF16),
        in_specs=[pl.BlockSpec(memory_space=pltpu.HBM)] * 2,
        out_specs=pl.BlockSpec(memory_space=VMEM),
        scratch_shapes=[
            pltpu.SMEM((SLOTS + 1,), jnp.int32),
            VMEM((C * ROWS, 128), F32),
            pltpu.SemaphoreType.DMA((2,)),
        ],
        name="pack",
        compiler_params=pltpu.CompilerParams(vmem_limit_bytes=LIMIT),
    )(*[pltpu.with_memory_space_constraint(v, pltpu.HBM) for v in (levels, x)])


def tables_kernel(levels_hbm, in_w_hbm, bias_hbm, cond_hbm, out_w_hbm, conv_hbm, film_ref, picks_ref, filter_ref, levels_ref, in_w_ref, bias_ref, cond_ref, out_w_ref, conv_ref, sems):
    sources = (levels_hbm, in_w_hbm, cond_hbm, out_w_hbm, bias_hbm, conv_hbm)
    targets = (levels_ref, in_w_ref, cond_ref, out_w_ref, bias_ref, conv_ref)
    copies = [pltpu.make_async_copy(a, b, sems.at[i]) for i, (a, b) in enumerate(zip(sources, targets))]
    for copy in copies:
        copy.start()
    to, frm = iota((256, 256), 0), iota((256, 256), 1)
    picks_ref[SWAP] = one_hot(((to >> 4) == (frm & 15)) & ((to & 15) == (frm >> 4)))
    to, frm = iota((128, 256), 0), iota((128, 256), 1) & 127
    picks_ref[BEFORE] = one_hot(((to >> 4) == (frm >> 4)) & ((frm & 15) < (to & 15)))
    cell = frm >> 4
    column = ((cell & 3) << 1) + (cell >> 2)
    picks_ref[UPTO] = one_hot(((to & 7) == column) & ((frm & 15) <= (to >> 3)))
    copies[0].wait()
    place = iota((SLOTS, 128), 0)
    now = jnp.zeros((SLOTS, 128), jnp.int32)
    following = now
    for k in range(SLOTS):
        now = jnp.where(place == k, levels_ref[k], now)
        following = jnp.where(place == k, levels_ref[k + 1], following)
    now, following = sigma_of(now), sigma_of(following)
    variance = now * now + 0.25
    root = jnp.sqrt(variance)
    ratio = (following - now) / now
    film_ref[4, :, :128] = 1.0 / root
    film_ref[4, :, 128:] = root
    film_ref[5, :, :128] = (1.0 - 0.25 / variance) * ratio
    film_ref[5, :, 128:] = 0.5 * now / root * ratio
    j = iota((SLOTS, 128), 1).astype(F32)
    frequency = jnp.exp(j * (jnp.log(F32(100.0)) / 128.0))
    phases = jnp.log(now) / 4.0 * frequency
    embedding = jnp.concatenate([jnp.cos(phases), jnp.sin(phases)], axis=1).astype(BF16)
    for copy in copies[1:5]:
        copy.wait()
    film_ref[6] = jnp.broadcast_to(bias_ref[...], (SLOTS, HID))
    conditions = jnp.dot(embedding, cond_ref[...], preferred_element_type=F32)
    film_ref[0] = 0.5 * (1.0 + conditions[:, 0:256])
    film_ref[1] = 0.5 * conditions[:, 256:512]
    film_ref[2] = 0.5 * (1.0 + conditions[:, 512:768])
    film_ref[3] = 0.5 * conditions[:, 768:1024]
    channel, lane = iota((C, 256), 0), iota((C, 256), 1)
    for row in range(ROWS):
        pick = one_hot(lane == lane_of(channel, row))
        packed = lax.dot_general(pick, in_w_ref[...], TN, preferred_element_type=F32)
        picks_ref[IN_PACK + 256 * row : IN_PACK + 256 * row + 256] = packed.astype(BF16)
    eye = one_hot(iota((C, 128), 0) == iota((C, 128), 1))
    picks_ref[IN_T] = lax.dot_general(eye, in_w_ref[...], TN, preferred_element_type=F32).astype(BF16)
    picks_ref[OUT_T] = lax.dot_general(eye, out_w_ref[...], TN, preferred_element_type=F32).astype(BF16)
    copies[5].wait()
    for layer in range(2):
        for a in range(3):
            west, mid, east = [conv_ref[layer, :, HID * (3 * a + b) : HID * (3 * a + b) + HID] for b in range(3)]
            lanes = slice(HID * a, HID * a + HID)
            outer = 0.5 * (west.astype(F32) + east.astype(F32))
            inner = 0.5 * mid.astype(F32)
            filter_ref[layer, 0, :, lanes] = west
            filter_ref[layer, 1, :, lanes] = (outer + inner).astype(BF16)
            filter_ref[layer, 2, :, lanes] = (outer - inner).astype(BF16)
            filter_ref[layer, 3, :, lanes] = east


def tables(levels, in_weight_t, in_bias, cond_weight, out_weight, conv_weight):
    return pl.pallas_call(
        tables_kernel,
        out_shape=[
            jax.ShapeDtypeStruct((7, SLOTS, HID), F32),
            jax.ShapeDtypeStruct((IN_PACK + 1024, 256), BF16),
            jax.ShapeDtypeStruct((2, 4, HID, 3 * HID), BF16),
        ],
        in_specs=[pl.BlockSpec(memory_space=pltpu.HBM)] * 6,
        out_specs=[pl.BlockSpec(memory_space=VMEM)] * 3,
        scratch_shapes=[
            pltpu.SMEM((SLOTS + 1,), jnp.int32),
            VMEM((C, HID), BF16),
            VMEM((1, HID), F32),
            VMEM((256, 1024), BF16),
            VMEM((C, HID), BF16),
            VMEM((2, HID, 9 * HID), BF16),
            pltpu.SemaphoreType.DMA((6,)),
        ],
        name="tables",
        compiler_params=pltpu.CompilerParams(vmem_limit_bytes=LIMIT),
    )(*[pltpu.with_memory_space_constraint(v, pltpu.HBM) for v in (levels, in_weight_t, in_bias, cond_weight, out_weight, conv_weight)])


def split(value):
    high = value.astype(BF16)
    return high, (value - high.astype(F32)).astype(BF16)


def convolve(view, rows, filters):
    parts = []
    for kind in range(4):
        views = [jnp.concatenate([view(kind, i + a) for i in rows], axis=0) for a in range(3)]
        lhs = jnp.concatenate(views, axis=1)
        parts.append(lax.dot_general(lhs, filters[kind], NT, preferred_element_type=F32))
    shape = (len(rows), parts[0].shape[0] // (len(rows) * SLOTS), SLOTS, HID)
    even = parts[0] + (parts[1] + parts[2])
    odd = (parts[1] - parts[2]) - parts[3]
    return even.reshape(shape), odd.reshape(shape)


def transform(ref, row, even, odd):
    size = (even.shape[0] - 1) * SLOTS
    values = (even[:-1] - even[1:], odd[:-1] + even[1:], even[1:] - odd[:-1], odd[:-1] - odd[1:])
    for kind, value in enumerate(values):
        ref[kind, row] = value.reshape(size, HID).astype(BF16)


def film(response, scale, shift):
    half = response * scale + shift
    return half * jnp.tanh(half) + half


def halves(value):
    high, low = split(value)
    return jnp.concatenate([high, low], axis=0)


def columns(value, count):
    pairs = value.reshape(count // 2, 2, SLOTS, value.shape[1])
    return pairs[:, 0], pairs[:, 1]


def scan(picks, drift):
    sums = []
    for start in range(0, drift.shape[0], 256):
        rhs = [halves(drift[start + at : start + at + 128]) for at in (0, 128)]
        both = jnp.dot(picks, jnp.concatenate(rhs, axis=1), preferred_element_type=F32)
        sums += [both[:, :128], both[:, 128:]]
    return sums


def ordered(values, picks_ref):
    blocks = [
        [value[:, 16 * group : 16 * group + 16, :].reshape(256, 128) for group in range(3)] for value in values
    ]
    swap = picks_ref[SWAP]
    heads = []
    for block in blocks:
        both = jnp.dot(swap, jnp.concatenate(block[:2], axis=1), preferred_element_type=F32)
        heads.append((both[:, :128], both[:, 128:]))
    tails = jnp.dot(swap, jnp.concatenate([block[2] for block in blocks], axis=1), preferred_element_type=F32)
    return heads, [tails[:, 128 * at : 128 * at + 128] for at in range(len(blocks))]


def project(heads, tails, row, picks_ref):
    lhs = [jnp.concatenate([head[row & 1], tail], axis=1).astype(BF16) for head, tail in zip(heads, tails)]
    weight = picks_ref[IN_PACK + 256 * row : IN_PACK + 256 * row + 256]
    hidden = jnp.dot(jnp.concatenate(lhs, axis=0), weight, preferred_element_type=F32)
    return [columns(hidden[256 * at : 256 * at + 256], 16) for at in range(len(heads))]


def state_of(head, tail, row, film_ref):
    head, tail = head[row & 1][32:224], tail[32:224]
    if row >= 2:
        head = pltpu.roll(head, 64, 1)
    if row != 2:
        tail = pltpu.roll(tail, (64 - 32 * row) % 128, 1)
    lane = iota((1, 128), 1)
    even, odd = columns(jnp.where(lane < 64, head, jnp.where(lane < C, tail, 0.0)), 12)
    root = film_ref[4, :, 128:][None]
    return even * root, odd * root


def inner_kernel(own_ref, film_ref, picks_ref, filter_ref, h0, h1, keep_ref, x_ref):
    heads, tails = ordered([own_ref[...]], picks_ref)
    shift = film_ref[6][None]
    for row in range(ROWS):
        even, odd = project(heads, tails, row, picks_ref)[0]
        transform(h0, row, even + shift, odd + shift)
        x_ref[0, row], x_ref[1, row] = state_of(heads[0], tails[0], row, film_ref)
    even, odd = convolve(lambda kind, i: h0[kind, i], (0, 1), filter_ref.at[0])
    even, odd = film(even, film_ref[0], film_ref[1]), film(odd, film_ref[0], film_ref[1])
    for at in range(2):
        transform(h1, at, even[at], odd[at])
        keep_ref[0, at], keep_ref[1, at] = odd[at, :-1].astype(BF16), even[at, 1:].astype(BF16)


def inner(own, prepared):
    return pl.pallas_call(
        inner_kernel,
        out_shape=[
            jax.ShapeDtypeStruct((4, ROWS, 112, HID), BF16),
            jax.ShapeDtypeStruct((4, 2, 96, HID), BF16),
            jax.ShapeDtypeStruct((2, 2, 6, SLOTS, HID), BF16),
            jax.ShapeDtypeStruct((2, ROWS, 6, SLOTS, 128), F32),
        ],
        in_specs=[pl.BlockSpec(memory_space=VMEM)] * 4,
        out_specs=[pl.BlockSpec(memory_space=VMEM)] * 4,
        name="inner",
        compiler_params=pltpu.CompilerParams(vmem_limit_bytes=LIMIT),
    )(own, *prepared)


def main_kernel(near_ref, far_ref, film_ref, picks_ref, filter_ref, h0_own, h1_own, keep_own, x_own, o_ref, h0, h1, g0, g1, h1_even, h1_odd, g1_even, g1_odd, x_even, x_odd, s_even, s_odd):
    place = lax.axis_index("lat")
    count = lax.axis_size("lat")
    inside_low = jnp.where(place > 0, 1.0, 0.0).astype(F32)
    inside_high = jnp.where(place < count - 1, 1.0, 0.0).astype(F32)
    gates = (inside_low, inside_high)
    bias = film_ref[6]
    inverse = film_ref[4, :, :128]
    keep, gain = film_ref[5, :, :128], film_ref[5, :, 128:]
    lane = iota((1, 128), 1)
    first = iota((1, 1, SLOTS, 128), 2) == 0

    def gate_of(row):
        return inside_low if row < 0 else inside_high if row >= ROWS else F32(1.0)

    swap_odd = (place & 1) == 1
    near, far = near_ref[...], far_ref[...]
    heads, tails = ordered([jnp.where(swap_odd, near, far), jnp.where(swap_odd, far, near)], picks_ref)
    for row in range(ROWS):
        for at, (even, odd) in enumerate(project(heads, tails, row, picks_ref)):
            shift = (bias * gates[at])[None]
            transform(h0, 4 * at + row, even + shift, odd + shift)
        at = 1 if row < 2 else 0
        i = 2 + row if row < 2 else row - 2
        x_even[i], x_odd[i] = state_of(heads[at], tails[at], row, film_ref)

    def view_zero(kind, i):
        return h0_own[kind, i - 4] if 4 <= i < 8 else h0[kind, i if i < 4 else i - 4]

    def view_one(kind, i):
        return h1_own[kind, i - 4] if 4 <= i < 6 else h1[kind, i if i < 4 else i - 2]

    for rows in (range(0, 4), range(6, 10)):
        even, odd = convolve(view_zero, rows, filter_ref.at[0])
        for at, i in enumerate(rows):
            to = i if i < 4 else i - 2
            scale, shift = film_ref[0] * gate_of(i - 3), film_ref[1] * gate_of(i - 3)
            here_even, here_odd = film(even[at], scale[None], shift[None]), film(odd[at], scale[None], shift[None])
            transform(h1, to, here_even, here_odd)
            if 1 <= i < 9:
                h1_even[to - 1] = here_odd[:-1].astype(BF16)
                h1_odd[to - 1] = here_even[1:].astype(BF16)

    def network(even, odd):
        hidden = jnp.concatenate([even.reshape(-1, HID), odd.reshape(-1, HID)], axis=0).astype(BF16)
        return lax.dot_general(hidden, picks_ref[OUT_T], NT, preferred_element_type=F32)

    film_two = film_ref[2][None, None], film_ref[3][None, None]

    for top in range(0, 8, 4):
        even, odd = convolve(view_one, range(top, top + 4), filter_ref.at[1])
        lower = top == 0

        def around(own, other):
            return jnp.concatenate([other, own] if lower else [own, other], axis=0).astype(F32)

        side = slice(0, 3) if lower else slice(3, 6)
        mine = slice(0, 1) if lower else slice(1, 2)
        even = around(keep_own[0, mine], h1_even[side]) + film(even, *film_two)
        odd = around(keep_own[1, mine], h1_odd[side]) + film(odd, *film_two)
        side, mine = (slice(0, 2), slice(0, 2)) if lower else (slice(2, 4), slice(2, 4))
        x = jnp.concatenate([around(x_own[0, mine], x_even[side]), around(x_own[1, mine], x_odd[side])], axis=0)
        anchor = jnp.where(first, x, 0.0)
        drift = keep * x - gain * network(even, odd).reshape(8, 6, SLOTS, 128) + anchor
        state = jnp.concatenate(scan(picks_ref[BEFORE], drift.reshape(768, 128)), axis=0)
        state = state.reshape(8, 6, SLOTS, 128) + anchor
        scaled = []
        for parity in range(2):
            for at in range(4):
                i = top + at
                here = state[4 * parity + at]
                if 2 <= i < 6:
                    if parity == 0:
                        s_even[i - 2] = here[1:5]
                    else:
                        s_odd[i - 2] = here[1:5]
                scaled.append((here * (inverse * gate_of(i - 2))[None]).reshape(96, 128).astype(BF16))
        hidden = jnp.dot(jnp.concatenate(scaled, axis=0), picks_ref[IN_T], preferred_element_type=F32)
        hidden = hidden.reshape(8, 6, SLOTS, HID)
        for at in range(4):
            shift = (bias * gate_of(top + at - 2))[None]
            transform(g0, top + at, hidden[at] + shift, hidden[4 + at] + shift)

    for top in range(0, 6, 3):
        even, odd = convolve(lambda kind, i: g0[kind, i], range(top, top + 3), filter_ref.at[0])
        for at in range(3):
            i = top + at
            scale, shift = film_ref[0] * gate_of(i - 1), film_ref[1] * gate_of(i - 1)
            here_even, here_odd = film(even[at], scale[None], shift[None]), film(odd[at], scale[None], shift[None])
            transform(g1, i, here_even, here_odd)
            if 1 <= i < 5:
                g1_even[i - 1] = here_odd[:-1].astype(BF16)
                g1_odd[i - 1] = here_even[1:].astype(BF16)

    even, odd = convolve(lambda kind, i: g1[kind, i], range(4), filter_ref.at[1])
    even = g1_even[...].astype(F32) + film(even, *film_two)
    odd = g1_odd[...].astype(F32) + film(odd, *film_two)
    state = jnp.concatenate([s_even[...], s_odd[...]], axis=0)
    drift = keep * state - gain * network(even, odd).reshape(8, 4, SLOTS, 128) + jnp.where(first, state, 0.0)
    drift = drift.reshape(2, 4, 64, 128)
    done = scan(picks_ref[UPTO], jnp.concatenate([drift[0], drift[1]], axis=1).reshape(512, 128))
    tail = pltpu.roll(done[0], 64, 1)
    for row in range(1, ROWS):
        here = done[row] if row == 2 else pltpu.roll(done[row], (32 * row - 64) % 128, 1)
        tail = jnp.where(lane < 32 * row, tail, here)
    for half in range(2):
        head = jnp.where(lane < 64, done[half], pltpu.roll(done[half + 2], 64, 1))
        o_ref[:, COLS * half : COLS * half + COLS, :] = head.reshape(SLOTS, COLS, 128).astype(BF16)
    o_ref[:, 2 * COLS :, :] = tail.reshape(SLOTS, COLS, 128).astype(BF16)


def main(near, far, prepared, middle):
    return pl.pallas_call(
        main_kernel,
        out_shape=jax.ShapeDtypeStruct((SLOTS, BACK, 128), BF16),
        in_specs=[pl.BlockSpec(memory_space=VMEM)] * 9,
        out_specs=pl.BlockSpec(memory_space=VMEM),
        scratch_shapes=[
            VMEM((4, 8, 112, HID), BF16),
            VMEM((4, 8, 96, HID), BF16),
            VMEM((4, 8, 80, HID), BF16),
            VMEM((4, 6, 64, HID), BF16),
            *[VMEM((6, 6, SLOTS, HID), BF16)] * 2,
            *[VMEM((ROWS, 4, SLOTS, HID), BF16)] * 2,
            *[VMEM((4, 6, SLOTS, 128), F32)] * 2,
            *[VMEM((ROWS, 4, SLOTS, 128), F32)] * 2,
        ],
        name="patch",
        compiler_params=pltpu.CompilerParams(vmem_limit_bytes=LIMIT),
    )(near, far, *prepared, *middle)


def unpack_kernel(p_ref, o_ref):
    pieces = p_ref[...].astype(F32)

    def turned(group):
        return pieces[:, COLS * group : COLS * group + COLS, :].reshape(128, 128).T

    heads, tail = [turned(0), turned(1)], turned(2)
    for row in range(ROWS):
        start = 64 if row >= 2 else 0
        o_ref[pl.ds(row, 64, stride=ROWS), :] = heads[row & 1][start : start + 64]
        o_ref[pl.ds(64 * ROWS + row, C - 64, stride=ROWS), :] = tail[32 * row : 32 * row + C - 64]


def unpack(pieces):
    return pl.pallas_call(
        unpack_kernel,
        out_shape=jax.ShapeDtypeStruct((C * ROWS, 128), F32),
        in_specs=[pl.BlockSpec(memory_space=VMEM)],
        out_specs=pl.BlockSpec(memory_space=VMEM),
        name="unpack",
        compiler_params=pltpu.CompilerParams(vmem_limit_bytes=LIMIT),
    )(pieces)


def on_device(trajectory, step_levels, in_weight, in_bias, conv_weight, cond_weight, out_weight):
    count = lax.axis_size("lat")
    near_pairs = [(i, i ^ 1) for i in range(count)]
    far_pairs = [pair for i in range(1, count - 1, 2) for pair in ((i, i + 1), (i + 1, i))]
    pieces = pack(step_levels, trajectory.reshape(C * ROWS, 128))
    own = lax.all_to_all(pieces, "tm", 0, 0)
    prepared = tables(step_levels, in_weight.T, in_bias[None, :], cond_weight, out_weight, conv_weight)
    own, prepared = lax.optimization_barrier((own, prepared))
    near = lax.ppermute(own, "lat", near_pairs)
    far = lax.ppermute(own, "lat", far_pairs)
    done = main(near, far, prepared, inner(own, prepared))
    back = lax.all_to_all(done, "tm", 0, 0)
    return unpack(back).reshape(1, C, ROWS, 128)


def solution(mesh):
    in_specs = (P("tm", None, "lat", None), P(), P(), P(), P(), P(), P())
    out_specs = P("tm", None, "lat", None)
    return jax.shard_map(on_device, mesh=mesh, in_specs=in_specs, out_specs=out_specs, check_vma=False)
```

```python
import functools

import jax
import jax.numpy as jnp
from jax import lax
from jax.experimental import pallas as pl
from jax.experimental.pallas import tpu as pltpu
from jax.sharding import PartitionSpec as P

LEVELS = 64
C = 84
HID = 256
SLOTS = 16
ROWS = 4
COLS = 8
PIECE = 48
BACK = 24
SWAP, BEFORE, UPTO, IN_T, OUT_T = slice(0, 256), slice(256, 384), slice(384, 512), slice(512, 640), slice(640, 768)
IN_PACK = 768
CONV_ONE = (((0, 1, 2, 3), (0, 1, 2), (0, 1)), ((8, 9), (7, 8, 9), (6, 7, 8, 9)))
CONV_TWO = (((0, 1, 2, 3), (0, 1, 2), (0, 1)), ((6, 7), (5, 6, 7), (4, 5, 6, 7)))
OWN_ONE = ((4, 5, 6, 7), (3, 4, 5, 6), (2, 3, 4, 5))
OWN_TWO = ((4, 5), (3, 4), (2, 3))
LIMIT = 32 << 20

SIGMA_TOP = 1.0
SIGMA_LOW = 0.02
RHO = 7.0
ROOT_TOP = SIGMA_TOP ** (1.0 / RHO)
ROOT_LOW = SIGMA_LOW ** (1.0 / RHO)

F32 = jnp.float32
BF16 = jnp.bfloat16
VMEM = pltpu.VMEM
NT = (((1,), (1,)), ((), ()))
TN = (((0,), (0,)), ((), ()))


def iota(shape, dim):
    return lax.broadcasted_iota(jnp.int32, shape, dim)


def one_hot(mask):
    return jnp.where(mask, 1.0, 0.0).astype(BF16)


def sigma_of(level):
    root = ROOT_TOP + level.astype(F32) / (LEVELS - 1) * (ROOT_LOW - ROOT_TOP)
    square = root * root
    return square * square * square * root


def lane_of(channel, row):
    head = channel + jnp.where(row >= 2, 64, 0)
    tail = 128 + 32 * row + (channel - 64)
    return jnp.where(channel < 64, head, tail)


def pack_kernel(levels_hbm, x_hbm, o_ref, levels_ref, x_ref, sems):
    get_levels = pltpu.make_async_copy(levels_hbm, levels_ref, sems.at[0])
    get_x = pltpu.make_async_copy(x_hbm, x_ref, sems.at[1])
    get_levels.start()
    get_x.start()
    slot = lax.axis_index("tm")
    shape = (C * ROWS, 3 * 128)
    index, lane = iota(shape, 0), iota(shape, 1)
    channel, row = index >> 2, index & 3
    target = lane_of(channel, row)
    target = jnp.where(target < 128, target + 128 * (row & 1), target + 128)
    places = one_hot(lane == target)
    get_levels.wait()
    sigma = sigma_of(jnp.full((1, 128), levels_ref[slot], jnp.int32))
    scale = jnp.sqrt(sigma * sigma + 0.25)
    get_x.wait()
    scaled = pltpu.roll(x_ref[...] / scale, 4, 1).astype(BF16)
    packed = lax.dot_general(scaled, places, TN, preferred_element_type=F32)
    for window in range(SLOTS):
        start = COLS * window
        if window < SLOTS - 1:
            part = packed[start : start + 2 * COLS]
        else:
            part = jnp.concatenate([packed[start:], packed[:COLS]], axis=0)
        part = part.astype(BF16)
        for group in range(3):
            o_ref[window, 16 * group : 16 * group + 16, :] = part[:, 128 * group : 128 * group + 128]


def pack(levels, x):
    return pl.pallas_call(
        pack_kernel,
        out_shape=jax.ShapeDtypeStruct((SLOTS, PIECE, 128), BF16),
        in_specs=[pl.BlockSpec(memory_space=pltpu.HBM)] * 2,
        out_specs=pl.BlockSpec(memory_space=VMEM),
        scratch_shapes=[
            pltpu.SMEM((SLOTS + 1,), jnp.int32),
            VMEM((C * ROWS, 128), F32),
            pltpu.SemaphoreType.DMA((2,)),
        ],
        name="pack",
        compiler_params=pltpu.CompilerParams(vmem_limit_bytes=LIMIT),
    )(*[pltpu.with_memory_space_constraint(v, pltpu.HBM) for v in (levels, x)])


def tables_kernel(levels_hbm, in_w_hbm, bias_hbm, cond_hbm, out_w_hbm, conv_hbm, film_ref, picks_ref, filter_ref, levels_ref, in_w_ref, bias_ref, cond_ref, out_w_ref, conv_ref, sems):
    sources = (levels_hbm, in_w_hbm, cond_hbm, out_w_hbm, bias_hbm, conv_hbm)
    targets = (levels_ref, in_w_ref, cond_ref, out_w_ref, bias_ref, conv_ref)
    copies = [pltpu.make_async_copy(a, b, sems.at[i]) for i, (a, b) in enumerate(zip(sources, targets))]
    for copy in copies:
        copy.start()
    to, frm = iota((256, 256), 0), iota((256, 256), 1)
    picks_ref[SWAP] = one_hot(((to >> 4) == (frm & 15)) & ((to & 15) == (frm >> 4)))
    to, frm = iota((128, 256), 0), iota((128, 256), 1) & 127
    picks_ref[BEFORE] = one_hot(((to >> 4) == (frm >> 4)) & ((frm & 15) < (to & 15)))
    cell = frm >> 4
    column = ((cell & 3) << 1) + (cell >> 2)
    picks_ref[UPTO] = one_hot(((to & 7) == column) & ((frm & 15) <= (to >> 3)))
    copies[0].wait()
    place = iota((SLOTS, 128), 0)
    now = jnp.zeros((SLOTS, 128), jnp.int32)
    following = now
    for k in range(SLOTS):
        now = jnp.where(place == k, levels_ref[k], now)
        following = jnp.where(place == k, levels_ref[k + 1], following)
    now, following = sigma_of(now), sigma_of(following)
    variance = now * now + 0.25
    root = jnp.sqrt(variance)
    ratio = (following - now) / now
    film_ref[4, :, :128] = 1.0 / root
    film_ref[4, :, 128:] = root
    film_ref[5, :, :128] = (1.0 - 0.25 / variance) * ratio
    film_ref[5, :, 128:] = 0.5 * now / root * ratio
    j = iota((SLOTS, 128), 1).astype(F32)
    frequency = jnp.exp(j * (jnp.log(F32(100.0)) / 128.0))
    phases = jnp.log(now) / 4.0 * frequency
    embedding = jnp.concatenate([jnp.cos(phases), jnp.sin(phases)], axis=1).astype(BF16)
    for copy in copies[1:5]:
        copy.wait()
    film_ref[6] = jnp.broadcast_to(bias_ref[...], (SLOTS, HID))
    conditions = jnp.dot(embedding, cond_ref[...], preferred_element_type=F32)
    film_ref[0] = 0.5 * (1.0 + conditions[:, 0:256])
    film_ref[1] = 0.5 * conditions[:, 256:512]
    film_ref[2] = 0.5 * (1.0 + conditions[:, 512:768])
    film_ref[3] = 0.5 * conditions[:, 768:1024]
    channel, lane = iota((C, 256), 0), iota((C, 256), 1)
    for row in range(ROWS):
        pick = one_hot(lane == lane_of(channel, row))
        packed = lax.dot_general(pick, in_w_ref[...], TN, preferred_element_type=F32)
        picks_ref[IN_PACK + 256 * row : IN_PACK + 256 * row + 256] = packed.astype(BF16)
    eye = one_hot(iota((C, 128), 0) == iota((C, 128), 1))
    picks_ref[IN_T] = lax.dot_general(eye, in_w_ref[...], TN, preferred_element_type=F32).astype(BF16)
    picks_ref[OUT_T] = lax.dot_general(eye, out_w_ref[...], TN, preferred_element_type=F32).astype(BF16)
    copies[5].wait()
    for layer in range(2):
        for a in range(3):
            west, mid, east = [conv_ref[layer, :, HID * (3 * a + b) : HID * (3 * a + b) + HID] for b in range(3)]
            lanes = slice(HID * a, HID * a + HID)
            outer = 0.5 * (west.astype(F32) + east.astype(F32))
            inner = 0.5 * mid.astype(F32)
            filter_ref[layer, 0, :, lanes] = west
            filter_ref[layer, 1, :, lanes] = (outer + inner).astype(BF16)
            filter_ref[layer, 2, :, lanes] = (outer - inner).astype(BF16)
            filter_ref[layer, 3, :, lanes] = east


def tables(levels, in_weight_t, in_bias, cond_weight, out_weight, conv_weight):
    return pl.pallas_call(
        tables_kernel,
        out_shape=[
            jax.ShapeDtypeStruct((7, SLOTS, HID), F32),
            jax.ShapeDtypeStruct((IN_PACK + 1024, 256), BF16),
            jax.ShapeDtypeStruct((2, 4, HID, 3 * HID), BF16),
        ],
        in_specs=[pl.BlockSpec(memory_space=pltpu.HBM)] * 6,
        out_specs=[pl.BlockSpec(memory_space=VMEM)] * 3,
        scratch_shapes=[
            pltpu.SMEM((SLOTS + 1,), jnp.int32),
            VMEM((C, HID), BF16),
            VMEM((1, HID), F32),
            VMEM((256, 1024), BF16),
            VMEM((C, HID), BF16),
            VMEM((2, HID, 9 * HID), BF16),
            pltpu.SemaphoreType.DMA((6,)),
        ],
        name="tables",
        compiler_params=pltpu.CompilerParams(vmem_limit_bytes=LIMIT),
    )(*[pltpu.with_memory_space_constraint(v, pltpu.HBM) for v in (levels, in_weight_t, in_bias, cond_weight, out_weight, conv_weight)])


def split(value):
    high = value.astype(BF16)
    return high, (value - high.astype(F32)).astype(BF16)


def convolve(view, rows, filters):
    parts = []
    for kind in range(4):
        views = [jnp.concatenate([view(kind, i + a) for i in rows], axis=0) for a in range(3)]
        lhs = jnp.concatenate(views, axis=1)
        parts.append(lax.dot_general(lhs, filters[kind], NT, preferred_element_type=F32))
    shape = (len(rows), parts[0].shape[0] // (len(rows) * SLOTS), SLOTS, HID)
    even = parts[0] + (parts[1] + parts[2])
    odd = (parts[1] - parts[2]) - parts[3]
    return even.reshape(shape), odd.reshape(shape)


def partial_responses(view, rows_of, filters):
    sums = []
    for kind in range(4):
        total = {}
        for a, rows in enumerate(rows_of):
            lhs = jnp.concatenate([view(kind, i + a) for i in rows], axis=0)
            weight = filters[kind, :, HID * a : HID * a + HID]
            out = lax.dot_general(lhs, weight, NT, preferred_element_type=F32)
            size = out.shape[0] // len(rows)
            for at, i in enumerate(rows):
                piece = out[size * at : size * at + size]
                total[i] = total[i] + piece if i in total else piece
        sums.append(total)
    result = {}
    for i in sums[0]:
        parts = [total[i].reshape(-1, SLOTS, HID) for total in sums]
        result[i] = parts[0] + (parts[1] + parts[2]), (parts[1] - parts[2]) - parts[3]
    return result


def transform(ref, row, even, odd):
    size = (even.shape[0] - 1) * SLOTS
    values = (even[:-1] - even[1:], odd[:-1] + even[1:], even[1:] - odd[:-1], odd[:-1] - odd[1:])
    for kind, value in enumerate(values):
        ref[kind, row] = value.reshape(size, HID).astype(BF16)


def film(response, scale, shift):
    half = response * scale + shift
    return half * jnp.tanh(half) + half


def halves(value):
    high, low = split(value)
    return jnp.concatenate([high, low], axis=0)


def columns(value, count):
    pairs = value.reshape(count // 2, 2, SLOTS, value.shape[1])
    return pairs[:, 0], pairs[:, 1]


def scan(picks, drift):
    sums = []
    for start in range(0, drift.shape[0], 256):
        rhs = [halves(drift[start + at : start + at + 128]) for at in (0, 128)]
        both = jnp.dot(picks, jnp.concatenate(rhs, axis=1), preferred_element_type=F32)
        sums += [both[:, :128], both[:, 128:]]
    return sums


def ordered(values, picks_ref):
    blocks = [
        [value[:, 16 * group : 16 * group + 16, :].reshape(256, 128) for group in range(3)] for value in values
    ]
    swap = picks_ref[SWAP]
    heads = []
    for block in blocks:
        both = jnp.dot(swap, jnp.concatenate(block[:2], axis=1), preferred_element_type=F32)
        heads.append((both[:, :128], both[:, 128:]))
    tails = jnp.dot(swap, jnp.concatenate([block[2] for block in blocks], axis=1), preferred_element_type=F32)
    return heads, [tails[:, 128 * at : 128 * at + 128] for at in range(len(blocks))]


def project(heads, tails, row, picks_ref):
    lhs = [jnp.concatenate([head[row & 1], tail], axis=1).astype(BF16) for head, tail in zip(heads, tails)]
    weight = picks_ref[IN_PACK + 256 * row : IN_PACK + 256 * row + 256]
    hidden = jnp.dot(jnp.concatenate(lhs, axis=0), weight, preferred_element_type=F32)
    return [columns(hidden[256 * at : 256 * at + 256], 16) for at in range(len(heads))]


def state_of(head, tail, row, film_ref):
    head, tail = head[row & 1][32:224], tail[32:224]
    if row >= 2:
        head = pltpu.roll(head, 64, 1)
    if row != 2:
        tail = pltpu.roll(tail, (64 - 32 * row) % 128, 1)
    lane = iota((1, 128), 1)
    even, odd = columns(jnp.where(lane < 64, head, jnp.where(lane < C, tail, 0.0)), 12)
    root = film_ref[4, :, 128:][None]
    return even * root, odd * root


def inner_kernel(own_ref, film_ref, picks_ref, filter_ref, h1, keep_ref, x_ref, part_one, part_two, h0):
    heads, tails = ordered([own_ref[...]], picks_ref)
    shift = film_ref[6][None]
    for row in range(ROWS):
        even, odd = project(heads, tails, row, picks_ref)[0]
        transform(h0, row, even + shift, odd + shift)
        x_ref[0, row], x_ref[1, row] = state_of(heads[0], tails[0], row, film_ref)
    found = partial_responses(lambda kind, i: h0[kind, i - 4], OWN_ONE, filter_ref.at[0])
    for at, i in enumerate((2, 3, 6, 7)):
        part_one[0, at], part_one[1, at] = found[i]
    for at in range(2):
        even, odd = [film(value, film_ref[0][None], film_ref[1][None]) for value in found[4 + at]]
        transform(h1, at, even, odd)
        keep_ref[0, at], keep_ref[1, at] = odd[:-1].astype(BF16), even[1:].astype(BF16)
    found = partial_responses(lambda kind, i: h1[kind, i - 4], OWN_TWO, filter_ref.at[1])
    for at in range(4):
        part_two[0, at], part_two[1, at] = found[2 + at]


def inner(own, prepared):
    return pl.pallas_call(
        inner_kernel,
        out_shape=[
            jax.ShapeDtypeStruct((4, 2, 96, HID), BF16),
            jax.ShapeDtypeStruct((2, 2, 6, SLOTS, HID), BF16),
            jax.ShapeDtypeStruct((2, ROWS, 6, SLOTS, 128), F32),
            jax.ShapeDtypeStruct((2, 4, 7, SLOTS, HID), F32),
            jax.ShapeDtypeStruct((2, 4, 6, SLOTS, HID), F32),
        ],
        in_specs=[pl.BlockSpec(memory_space=VMEM)] * 4,
        out_specs=[pl.BlockSpec(memory_space=VMEM)] * 5,
        scratch_shapes=[VMEM((4, ROWS, 112, HID), BF16)],
        name="inner",
        compiler_params=pltpu.CompilerParams(vmem_limit_bytes=LIMIT),
    )(own, *prepared)


def main_kernel(near_ref, far_ref, film_ref, picks_ref, filter_ref, h1_own, keep_own, x_own, part_one, part_two, o_ref, h0, h1, g0, g1, h1_even, h1_odd, g1_even, g1_odd, x_even, x_odd, s_even, s_odd):
    place = lax.axis_index("lat")
    count = lax.axis_size("lat")
    inside_low = jnp.where(place > 0, 1.0, 0.0).astype(F32)
    inside_high = jnp.where(place < count - 1, 1.0, 0.0).astype(F32)
    gates = (inside_low, inside_high)
    bias = film_ref[6]
    inverse = film_ref[4, :, :128]
    keep, gain = film_ref[5, :, :128], film_ref[5, :, 128:]
    lane = iota((1, 128), 1)
    first = iota((1, 1, SLOTS, 128), 2) == 0

    def gate_of(row):
        return inside_low if row < 0 else inside_high if row >= ROWS else F32(1.0)

    swap_odd = (place & 1) == 1
    near, far = near_ref[...], far_ref[...]
    heads, tails = ordered([jnp.where(swap_odd, near, far), jnp.where(swap_odd, far, near)], picks_ref)
    for row in range(ROWS):
        for at, (even, odd) in enumerate(project(heads, tails, row, picks_ref)):
            shift = (bias * gates[at])[None]
            transform(h0, 4 * at + row, even + shift, odd + shift)
        at = 1 if row < 2 else 0
        i = 2 + row if row < 2 else row - 2
        x_even[i], x_odd[i] = state_of(heads[at], tails[at], row, film_ref)

    def view_zero(kind, i):
        return h0[kind, i if i < 4 else i - 4]

    def view_one(kind, i):
        return h1[kind, i if i < 4 else i - 2]

    def with_own(found, i, rows, part):
        if i not in rows:
            return found[i]
        at = rows.index(i)
        return found[i][0] + part[0, at], found[i][1] + part[1, at]

    for rows_of in CONV_ONE:
        found = partial_responses(view_zero, rows_of, filter_ref.at[0])
        for i in sorted(found):
            to = i if i < 4 else i - 2
            even, odd = with_own(found, i, (2, 3, 6, 7), part_one)
            scale, shift = (film_ref[0] * gate_of(i - 3))[None], (film_ref[1] * gate_of(i - 3))[None]
            here_even, here_odd = film(even, scale, shift), film(odd, scale, shift)
            transform(h1, to, here_even, here_odd)
            if 1 <= i < 9:
                h1_even[to - 1] = here_odd[:-1].astype(BF16)
                h1_odd[to - 1] = here_even[1:].astype(BF16)

    def network(even, odd):
        hidden = jnp.concatenate([even.reshape(-1, HID), odd.reshape(-1, HID)], axis=0).astype(BF16)
        return lax.dot_general(hidden, picks_ref[OUT_T], NT, preferred_element_type=F32)

    film_two = film_ref[2][None, None], film_ref[3][None, None]

    def stacked(pick, rows):
        return jnp.concatenate([pick(r)[None] for r in rows], axis=0)

    def kept(parity, r):
        if 3 <= r < 5:
            return keep_own[parity, r - 3].astype(F32)
        return (h1_even, h1_odd)[parity][r if r < 3 else r - 2].astype(F32)

    def x_of(parity, r):
        return x_own[parity, r - 2] if 2 <= r < 6 else (x_even, x_odd)[parity][r if r < 2 else r - 4]

    for rows_of in CONV_TWO:
        found = partial_responses(view_one, rows_of, filter_ref.at[1])
        rows = sorted(found)
        n = len(rows)
        sums = [with_own(found, r, (2, 3, 4, 5), part_two) for r in rows]
        even, odd = [jnp.concatenate([pair[parity][None] for pair in sums], axis=0) for parity in range(2)]
        even = stacked(lambda r: kept(0, r), rows) + film(even, *film_two)
        odd = stacked(lambda r: kept(1, r), rows) + film(odd, *film_two)
        x = jnp.concatenate([stacked(lambda r: x_of(0, r), rows), stacked(lambda r: x_of(1, r), rows)], axis=0)
        anchor = jnp.where(first, x, 0.0)
        drift = keep * x - gain * network(even, odd).reshape(2 * n, 6, SLOTS, 128) + anchor
        drift = drift.reshape(n * 192, 128)
        state = jnp.concatenate(scan(picks_ref[BEFORE], drift), axis=0)
        state = state.reshape(2 * n, 6, SLOTS, 128) + anchor
        scaled = []
        for parity in range(2):
            for at, i in enumerate(rows):
                here = state[n * parity + at]
                if 2 <= i < 6:
                    if parity == 0:
                        s_even[i - 2] = here[1:5]
                    else:
                        s_odd[i - 2] = here[1:5]
                scaled.append((here * (inverse * gate_of(i - 2))[None]).reshape(96, 128).astype(BF16))
        hidden = jnp.dot(jnp.concatenate(scaled, axis=0), picks_ref[IN_T], preferred_element_type=F32)
        hidden = hidden.reshape(2 * n, 6, SLOTS, HID)
        for at, i in enumerate(rows):
            shift = (bias * gate_of(i - 2))[None]
            transform(g0, i, hidden[at] + shift, hidden[n + at] + shift)

    for top in range(0, 6, 3):
        even, odd = convolve(lambda kind, i: g0[kind, i], range(top, top + 3), filter_ref.at[0])
        for at in range(3):
            i = top + at
            scale, shift = film_ref[0] * gate_of(i - 1), film_ref[1] * gate_of(i - 1)
            here_even, here_odd = film(even[at], scale[None], shift[None]), film(odd[at], scale[None], shift[None])
            transform(g1, i, here_even, here_odd)
            if 1 <= i < 5:
                g1_even[i - 1] = here_odd[:-1].astype(BF16)
                g1_odd[i - 1] = here_even[1:].astype(BF16)

    even, odd = convolve(lambda kind, i: g1[kind, i], range(4), filter_ref.at[1])
    even = g1_even[...].astype(F32) + film(even, *film_two)
    odd = g1_odd[...].astype(F32) + film(odd, *film_two)
    state = jnp.concatenate([s_even[...], s_odd[...]], axis=0)
    drift = keep * state - gain * network(even, odd).reshape(8, 4, SLOTS, 128) + jnp.where(first, state, 0.0)
    drift = drift.reshape(2, 4, 64, 128)
    done = scan(picks_ref[UPTO], jnp.concatenate([drift[0], drift[1]], axis=1).reshape(512, 128))
    tail = pltpu.roll(done[0], 64, 1)
    for row in range(1, ROWS):
        here = done[row] if row == 2 else pltpu.roll(done[row], (32 * row - 64) % 128, 1)
        tail = jnp.where(lane < 32 * row, tail, here)
    for half in range(2):
        head = jnp.where(lane < 64, done[half], pltpu.roll(done[half + 2], 64, 1))
        o_ref[:, COLS * half : COLS * half + COLS, :] = head.reshape(SLOTS, COLS, 128).astype(BF16)
    o_ref[:, 2 * COLS :, :] = tail.reshape(SLOTS, COLS, 128).astype(BF16)


def main(near, far, prepared, middle):
    return pl.pallas_call(
        main_kernel,
        out_shape=jax.ShapeDtypeStruct((SLOTS, BACK, 128), BF16),
        in_specs=[pl.BlockSpec(memory_space=VMEM)] * 10,
        out_specs=pl.BlockSpec(memory_space=VMEM),
        scratch_shapes=[
            VMEM((4, 8, 112, HID), BF16),
            VMEM((4, 8, 96, HID), BF16),
            VMEM((4, 8, 80, HID), BF16),
            VMEM((4, 6, 64, HID), BF16),
            *[VMEM((6, 6, SLOTS, HID), BF16)] * 2,
            *[VMEM((ROWS, 4, SLOTS, HID), BF16)] * 2,
            *[VMEM((4, 6, SLOTS, 128), F32)] * 2,
            *[VMEM((ROWS, 4, SLOTS, 128), F32)] * 2,
        ],
        name="patch",
        compiler_params=pltpu.CompilerParams(vmem_limit_bytes=LIMIT),
    )(near, far, *prepared, *middle)


def unpack_kernel(p_ref, o_ref):
    pieces = p_ref[...].astype(F32)

    def turned(group):
        return pieces[:, COLS * group : COLS * group + COLS, :].reshape(128, 128).T

    heads, tail = [turned(0), turned(1)], turned(2)
    for row in range(ROWS):
        start = 64 if row >= 2 else 0
        o_ref[pl.ds(row, 64, stride=ROWS), :] = heads[row & 1][start : start + 64]
        o_ref[pl.ds(64 * ROWS + row, C - 64, stride=ROWS), :] = tail[32 * row : 32 * row + C - 64]


def unpack(pieces):
    return pl.pallas_call(
        unpack_kernel,
        out_shape=jax.ShapeDtypeStruct((C * ROWS, 128), F32),
        in_specs=[pl.BlockSpec(memory_space=VMEM)],
        out_specs=pl.BlockSpec(memory_space=VMEM),
        name="unpack",
        compiler_params=pltpu.CompilerParams(vmem_limit_bytes=LIMIT),
    )(pieces)


def on_device(trajectory, step_levels, in_weight, in_bias, conv_weight, cond_weight, out_weight):
    count = lax.axis_size("lat")
    near_pairs = [(i, i ^ 1) for i in range(count)]
    far_pairs = [pair for i in range(1, count - 1, 2) for pair in ((i, i + 1), (i + 1, i))]
    pieces = pack(step_levels, trajectory.reshape(C * ROWS, 128))
    own = lax.all_to_all(pieces, "tm", 0, 0)
    prepared = tables(step_levels, in_weight.T, in_bias[None, :], cond_weight, out_weight, conv_weight)
    own, prepared = lax.optimization_barrier((own, prepared))
    near = lax.ppermute(own, "lat", near_pairs)
    far = lax.ppermute(own, "lat", far_pairs)
    done = main(near, far, prepared, inner(own, prepared))
    back = lax.all_to_all(done, "tm", 0, 0)
    return unpack(back).reshape(1, C, ROWS, 128)


def solution(mesh):
    in_specs = (P("tm", None, "lat", None), P(), P(), P(), P(), P(), P())
    out_specs = P("tm", None, "lat", None)
    return jax.shard_map(on_device, mesh=mesh, in_specs=in_specs, out_specs=out_specs, check_vma=False)
```
